768 devices in a mesh: tensor: 48 (over y_hi, z), context: 16 (over x, y_lo, core).
Axes of the slice: x: 4, y: 8 (y_hi: 4, y_lo: 2; y = y_hi * 2 + y_lo), z: 12, core: 2. Of those that a mesh axis runs over, the one named last changes fastest.
Arguments:
- tokens: bfloat16 [6144, 8192], P('context'), may hold values from -48 to 48
- w_query: bfloat16 [8192, 6144], P(None, 'tensor'), may hold values from -0.0625 to 0.0625
- w_key: bfloat16 [8192, 6144], P(None, 'tensor'), may hold values from -0.0625 to 0.0625
- w_value: bfloat16 [8192, 6144], P(None, 'tensor'), may hold values from -0.0625 to 0.0625
- mix_gate: bfloat16 [48, 96], replicated, may hold values from -0.875 to 0.875
- mix_up: bfloat16 [48, 96], replicated, may hold values from -0.875 to 0.875
- mix_down: bfloat16 [96, 48], replicated, may hold values from -0.625 to 0.625
- block_ids: int32 [64], P('context'), may hold values from 0 to 31, as said below
Outputs:
- attended: bfloat16 [6144, 6144], P('context', 'tensor')
The draws below stay inside these ranges and needn't reach their ends.
Inputs may be any that keep to these rules, and one draw needn't show every extreme that they name: `block_ids`: device c of the context axis holds entries 4c to 4c+3: (a, 31 - a) for the first sequence and (b, 31 - b) for the second; over all devices each sequence's block numbers appear once each.
All inputs are finite; a program needn't handle non-finite values.
Results may differ from the reference program's by a relative error of at most 0.012.
The reference program's roundings to bfloat16 on the way (of `queries`, `hidden` and `mixed`) count: a program that leaves them out, or rounds other values in their place, can miss the bound.
Values may be sent and summed in bfloat16 or wider, within the bound.
No kernel may reach another device: no remote copies, remote signals or barrier semaphores. Data moves between devices by JAX's collectives and lax.ppermute only.
A program may use at most 64 MiB of HBM per device.

```python
import jax
import jax.numpy as jnp
from jax import lax

D = 8192
HEAD_DIM = 128
BLK = 96
HEADS = 48
MIXF = 96
TOKENS = 6144
N_CONTEXT = 16


def draw_tokens(key, part):
    base = jax.random.truncated_normal(key, -6.0, 6.0, (TOKENS, D), jnp.float32)
    return base.astype(jnp.bfloat16)


def draw_block_ids(key, part):
    firsts = jnp.stack([jax.random.permutation(jax.random.fold_in(key, 11 + s), N_CONTEXT) for s in range(2)], axis=1)
    firsts = firsts.astype(jnp.int32)
    paired = jnp.stack([firsts, 2 * N_CONTEXT - 1 - firsts], axis=2)
    return paired.reshape(4 * N_CONTEXT).astype(jnp.int32)


def block_scale(rng, extent, cuts, smallest, high):
    loudness, own = 1.0, jax.random.fold_in(rng, 6)
    for axis_at, parts in cuts:
        heights = jnp.exp(jax.random.uniform(jax.random.fold_in(own, axis_at), (parts,), jnp.float32, smallest / len(cuts), high / len(cuts)))
        loudness = loudness * jnp.repeat(heights, extent[axis_at] // parts).reshape([-1 if axis == axis_at else 1 for axis in range(len(extent))])
    return loudness


def gaussian(key, dims, scale, most, shards=(), kind=jnp.bfloat16):
    level = block_scale(key, dims, shards, -0.22, 0.18) if shards else 1.0
    values = jax.random.normal(key, dims, jnp.float32) * scale * level
    return jnp.minimum(jnp.maximum(values, -most), most).astype(kind)


def setup_inputs(seed: int = 0) -> dict:
    arg_keys = jax.random.split(jax.random.key(seed), 9)
    tokens = draw_tokens(jax.random.fold_in(arg_keys[8], 71), 0)
    w_query = gaussian(arg_keys[1], (D, HEADS * HEAD_DIM), D ** -0.5, 0.0625, ((1, 48),))
    w_key = gaussian(arg_keys[2], (D, HEADS * HEAD_DIM), D ** -0.5, 0.0625, ((1, 48),))
    w_value = gaussian(arg_keys[3], (D, HEADS * HEAD_DIM), D ** -0.5, 0.0625, ((1, 48),))
    mix_gate = gaussian(arg_keys[4], (HEADS, MIXF), HEADS ** -0.5, 0.875)
    mix_up = gaussian(arg_keys[5], (HEADS, MIXF), HEADS ** -0.5, 0.875)
    mix_down = gaussian(arg_keys[6], (MIXF, HEADS), MIXF ** -0.5, 0.625)
    block_ids = draw_block_ids(jax.random.fold_in(arg_keys[8], 71), 0)
    return dict(tokens=tokens, w_query=w_query, w_key=w_key, w_value=w_value, mix_gate=mix_gate, mix_up=mix_up, mix_down=mix_down, block_ids=block_ids)


def reference(tokens, w_query, w_key, w_value, mix_gate, mix_up, mix_down, block_ids):
    row_index = jnp.arange(TOKENS, dtype=jnp.int32)
    block_of = row_index // BLK
    positions = jnp.take(block_ids, block_of).astype(jnp.int32) * BLK + row_index % BLK
    seq_index = (block_of % 4) // 2
    queries = jnp.dot(tokens, w_query, preferred_element_type=jnp.float32).astype(jnp.bfloat16).reshape(TOKENS, HEADS, HEAD_DIM)
    keys_all = jnp.dot(tokens, w_key, preferred_element_type=jnp.float32).astype(jnp.bfloat16).reshape(TOKENS, HEADS, HEAD_DIM)
    values_all = jnp.dot(tokens, w_value, preferred_element_type=jnp.float32).astype(jnp.bfloat16).reshape(TOKENS, HEADS, HEAD_DIM)
    value_float = values_all.astype(jnp.float32)
    gate_part = jnp.einsum("thc,hf->tcf", value_float, mix_gate.astype(jnp.float32))
    up_part = jnp.einsum("thc,hf->tcf", value_float, mix_up.astype(jnp.float32))
    hidden = (jax.nn.silu(gate_part) * up_part).astype(jnp.bfloat16)
    mixing = jnp.einsum("tcf,fh->thc", hidden.astype(jnp.float32), mix_down.astype(jnp.float32))
    mixed = (value_float + mixing).astype(jnp.bfloat16)
    allowed = (seq_index[:, None] == seq_index[None, :]) & (positions[None, :] <= positions[:, None])
    scale = HEAD_DIM ** -0.5

    def one_head(operands):
        q_head, k_head, v_head = operands
        scores = jnp.dot(q_head, k_head.T, preferred_element_type=jnp.float32) * scale
        scores = jnp.where(allowed, scores, -1e30)
        top = jnp.max(scores, axis=1, keepdims=True)
        weights = jnp.where(allowed, jnp.exp(scores - top), 0.0)
        total = jnp.sum(weights, axis=1, keepdims=True)
        summed = jnp.dot(weights.astype(jnp.bfloat16), v_head, preferred_element_type=jnp.float32)
        return (summed / total).astype(jnp.bfloat16)

    heads_out = lax.map(one_head, (queries.transpose(1, 0, 2), keys_all.transpose(1, 0, 2), mixed.transpose(1, 0, 2)))
    return heads_out.transpose(1, 0, 2).reshape(TOKENS, HEADS * HEAD_DIM)
```

```python
import jax
import jax.numpy as jnp
from jax import lax
from jax.experimental import pallas as pl
from jax.experimental.pallas import tpu as pltpu
from jax.sharding import PartitionSpec as P


HEAD_DIM = 128
BLK = 96
PAD = 16
CORE_GROUPS = [[2 * k + core for k in range(8)] for core in range(2)]
VMEM = pltpu.MemorySpace.VMEM
SMEM = pltpu.MemorySpace.SMEM


def on_chip(x):
    return pltpu.with_memory_space_constraint(x, VMEM)


def value_kernel(x_ref, w_ref, out_ref, acc_ref):
    step = pl.program_id(0)
    part = jnp.dot(x_ref[...], w_ref[...], preferred_element_type=jnp.float32)

    @pl.when(step == 0)
    def _():
        acc_ref[...] = part

    @pl.when(step > 0)
    def _():
        acc_ref[...] += part

    @pl.when(step == pl.num_programs(0) - 1)
    def _():
        out_ref[...] = acc_ref[...].astype(out_ref.dtype)


def project_values(tokens, w_value, depth=2048):
    rows, width = tokens.shape
    cols = w_value.shape[1]
    return pl.pallas_call(
        value_kernel,
        grid=(width // depth,),
        in_specs=[
            pl.BlockSpec((rows, depth), lambda k: (0, k)),
            pl.BlockSpec((depth, cols), lambda k: (k, 0)),
        ],
        out_specs=pl.BlockSpec((rows, cols), lambda k: (0, 0)),
        out_shape=jax.ShapeDtypeStruct((rows, cols), jnp.bfloat16),
        scratch_shapes=[pltpu.VMEM((rows, cols), jnp.float32)],
        name="project_values",
    )(tokens, w_value)


def query_key_kernel(ids_ref, x_ref, wq_ref, wk_ref, q_ref, k_ref, acc_ref):
    step = pl.program_id(0)
    rows = x_ref.shape[0]
    cols = wq_ref.shape[1]
    both = jnp.concatenate([wq_ref[...], wk_ref[...]], axis=1)
    part = jnp.dot(x_ref[...], both, preferred_element_type=jnp.float32)

    @pl.when(step == 0)
    def _():
        acc_ref[...] = part

    @pl.when(step > 0)
    def _():
        acc_ref[...] += part

    @pl.when(step == pl.num_programs(0) - 1)
    def _():
        q_ref[...] = acc_ref[:, :cols].astype(q_ref.dtype)
        keys = acc_ref[:, cols:].astype(k_ref.dtype)
        row = lax.broadcasted_iota(jnp.int32, (PAD, cols), 0)
        ids = jnp.zeros((PAD, cols), jnp.float32)
        for j in range(4):
            ids = jnp.where(row == j, ids_ref[j].astype(jnp.float32), ids)
        k_ref[0, :rows, :] = keys
        k_ref[0, rows:, :] = ids.astype(k_ref.dtype)


def project_queries_keys(block_ids, tokens, w_query, w_key, depth=2048):
    rows, width = tokens.shape
    cols = w_query.shape[1]
    return pl.pallas_call(
        query_key_kernel,
        grid=(width // depth,),
        in_specs=[
            pl.BlockSpec(memory_space=SMEM),
            pl.BlockSpec((rows, depth), lambda k: (0, k)),
            pl.BlockSpec((depth, cols), lambda k: (k, 0)),
            pl.BlockSpec((depth, cols), lambda k: (k, 0)),
        ],
        out_specs=[
            pl.BlockSpec((rows, cols), lambda k: (0, 0)),
            pl.BlockSpec((1, rows + PAD, cols), lambda k: (0, 0, 0)),
        ],
        out_shape=[
            jax.ShapeDtypeStruct((rows, cols), jnp.bfloat16),
            jax.ShapeDtypeStruct((1, rows + PAD, cols), jnp.bfloat16),
        ],
        scratch_shapes=[pltpu.VMEM((rows, 2 * cols), jnp.float32)],
        name="project_queries_keys",
    )(block_ids, tokens, w_query, w_key)


def mix_kernel(u_ref, w_in_ref, w_out_ref, out_ref, wide_ref):
    count = u_ref.shape[1]
    hidden_units = w_in_ref.shape[0] // 2
    wide_ref[...] = u_ref[...].astype(jnp.float32)
    flat = jnp.concatenate([wide_ref[:, t, :] for t in range(count)], axis=1)
    parts = jnp.dot(w_in_ref[...], flat.astype(jnp.bfloat16), preferred_element_type=jnp.float32)
    hidden = (jax.nn.silu(parts[:hidden_units]) * parts[hidden_units:]).astype(jnp.bfloat16)
    mixed = flat + jnp.dot(w_out_ref[...], hidden, preferred_element_type=jnp.float32)
    for t in range(count):
        wide_ref[:, t, :] = mixed[:, t * HEAD_DIM : (t + 1) * HEAD_DIM]
    out_ref[...] = wide_ref[...].astype(out_ref.dtype)


def mix(gathered, w_in, w_out):
    return pl.pallas_call(
        mix_kernel,
        in_specs=[pl.BlockSpec(memory_space=VMEM)] * 3,
        out_specs=pl.BlockSpec(memory_space=VMEM),
        out_shape=jax.ShapeDtypeStruct(gathered.shape, jnp.bfloat16),
        scratch_shapes=[pltpu.VMEM(gathered.shape, jnp.float32)],
        name="mix_heads",
    )(on_chip(gathered), w_in, w_out)


def weight_kernel(ids_ref, q_ref, k0_ref, k1_ref, k2_ref, k3_ref, w_ref, total_ref, s_ref):
    half = q_ref.shape[0] // 2
    rows = q_ref.shape[0]
    chunk = 2 * half
    scale = HEAD_DIM ** (-0.5)
    q_row = lax.broadcasted_iota(jnp.int32, (half, 1), 0)
    lane = lax.broadcasted_iota(jnp.int32, (1, chunk), 1)
    lane_off = lane % BLK
    lane_blk = lane // BLK
    for s in range(2):
        id_lo, id_hi = ids_ref[2 * s], ids_ref[2 * s + 1]
        q_pos = jnp.where(q_row < BLK, id_lo * BLK + q_row, id_hi * BLK + q_row - BLK)
        queries = q_ref[s * half : (s + 1) * half, :]
        top = jnp.full((half, chunk), -1e30, jnp.float32)
        at = 0
        for k_ref in (k0_ref, k1_ref, k2_ref, k3_ref):
            for d in range(0, k_ref.shape[0], 2):
                keys = jnp.concatenate(
                    [k_ref[d + e, s * half : (s + 1) * half, :] for e in range(2)], axis=0
                )
                k_ids = jnp.zeros((1, chunk), jnp.float32)
                for e in range(2):
                    tail = k_ref[d + e, rows:, :].astype(jnp.float32)
                    for j in range(2):
                        wide = jnp.concatenate([tail[2 * s + j : 2 * s + j + 1, :]] * 3, axis=1)
                        k_ids = jnp.where(lane_blk == 2 * e + j, wide, k_ids)
                k_pos = k_ids.astype(jnp.int32) * BLK + lane_off
                scores = (
                    lax.dot_general(
                        queries, keys, (((1,), (1,)), ((), ())), preferred_element_type=jnp.float32
                    )
                    * scale
                )
                scores = jnp.where(k_pos <= q_pos, scores, -1e30)
                s_ref[:, at : at + chunk] = scores
                top = jnp.maximum(top, scores)
                at += chunk
        top = jnp.max(top, axis=1, keepdims=True)
        total = jnp.zeros((half, chunk), jnp.float32)
        for at in range(0, s_ref.shape[1], chunk):
            weights = jnp.exp(s_ref[:, at : at + chunk] - top)
            total = total + weights
            w_ref[s, :, at : at + chunk] = weights.astype(w_ref.dtype)
        total = jnp.sum(total, axis=1, keepdims=True)
        total_ref[s * half : (s + 1) * half, :] = jnp.broadcast_to(total, (half, HEAD_DIM))


def attention_weights(block_ids, queries, keys):
    rows = queries.shape[0]
    half = rows // 2
    count = sum(piece.shape[0] for piece in keys) * half
    return pl.pallas_call(
        weight_kernel,
        in_specs=[pl.BlockSpec(memory_space=SMEM)] + [pl.BlockSpec(memory_space=VMEM)] * 5,
        out_specs=[pl.BlockSpec(memory_space=VMEM)] * 2,
        out_shape=[
            jax.ShapeDtypeStruct((2, half, count), jnp.bfloat16),
            jax.ShapeDtypeStruct((rows, HEAD_DIM), jnp.float32),
        ],
        scratch_shapes=[pltpu.VMEM((half, count), jnp.float32)],
        name="attention_weights",
    )(block_ids, queries, *[on_chip(piece) for piece in keys])


def apply_kernel(spot_ref, w_ref, total_ref, v0_ref, v1_ref, out_ref):
    half = out_ref.shape[0] // 2
    sources = 4
    for s in range(2):
        acc = jnp.zeros((half, HEAD_DIM), jnp.float32)
        at = 0
        for v_ref in (v0_ref, v1_ref):
            for d in range(0, v_ref.shape[0], sources):
                values = jnp.concatenate(
                    [v_ref[spot_ref[d + e], s * half : (s + 1) * half, :] for e in range(sources)],
                    axis=0,
                )
                acc = acc + jnp.dot(
                    w_ref[s, :, at : at + sources * half],
                    values,
                    preferred_element_type=jnp.float32,
                )
                at += sources * half
        total = total_ref[s * half : (s + 1) * half, :]
        out_ref[s * half : (s + 1) * half, :] = (acc / total).astype(out_ref.dtype)


def apply_weights(spots, weights, total, values_mine, values_other):
    return pl.pallas_call(
        apply_kernel,
        in_specs=[pl.BlockSpec(memory_space=SMEM)] + [pl.BlockSpec(memory_space=VMEM)] * 4,
        out_specs=pl.BlockSpec(memory_space=VMEM),
        out_shape=jax.ShapeDtypeStruct(total.shape, jnp.bfloat16),
        name="apply_weights",
    )(spots, weights, total, on_chip(values_mine), on_chip(values_other))


def shards(tokens, w_query, w_key, w_value, mix_gate, mix_up, mix_down, block_ids):
    heads = mix_gate.shape[0]
    rows = tokens.shape[0]

    def exchange(x):
        return lax.all_to_all(x, "tensor", split_axis=0, concat_axis=0, tiled=True)

    def spread(x):
        return lax.all_to_all(
            x, "context", split_axis=0, concat_axis=0, axis_index_groups=CORE_GROUPS, tiled=True
        )

    def flip(x, bit):
        return lax.ppermute(x, "context", [(i, i ^ bit) for i in range(16)])

    def doubled(x, bit):
        return jnp.concatenate([x, flip(x, bit)], axis=0)

    w_in = jnp.concatenate([mix_gate, mix_up], axis=1).T
    w_out = mix_down.T
    values = project_values(tokens, w_value)
    gathered = exchange(values.reshape(heads, rows // heads, HEAD_DIM))
    tokens, values = lax.optimization_barrier((tokens, values))
    queries, keys = project_queries_keys(block_ids, tokens, w_query, w_key)
    keys = doubled(keys, 2)
    keys = doubled(keys, 8)
    near = flip(keys, 4)
    keys = [keys, near, flip(keys, 1), flip(near, 1)]
    turn = jnp.arange(8, dtype=jnp.int32)
    spots = (lax.axis_index("context") // 2) ^ (turn % 2 + turn // 2 % 2 * 4 + turn // 4 * 2)
    mixed = mix(gathered, w_in, w_out)
    mixed_rows = exchange(mixed).reshape(1, rows, HEAD_DIM)
    weights, total = attention_weights(block_ids, queries, keys)
    values_mine = spread(jnp.broadcast_to(mixed_rows, (8, rows, HEAD_DIM)))
    values_other = flip(values_mine, 1)
    return apply_weights(spots, weights, total, values_mine, values_other)


def solution(mesh):
    in_specs = (
        P("context", None),
        P(None, "tensor"),
        P(None, "tensor"),
        P(None, "tensor"),
        P(),
        P(),
        P(),
        P("context"),
    )
    out_specs = P("context", "tensor")
    return jax.shard_map(shards, mesh=mesh, in_specs=in_specs, out_specs=out_specs, check_vma=False)
```

```python
import jax
import jax.numpy as jnp
from jax import lax
from jax.experimental import pallas as pl
from jax.experimental.pallas import tpu as pltpu
from jax.sharding import PartitionSpec as P


HEAD_DIM = 128
BLK = 96
PAD = 16
CHUNKS = 8
CORE_GROUPS = [[2 * k + core for k in range(8)] for core in range(2)]
VMEM = pltpu.MemorySpace.VMEM
SMEM = pltpu.MemorySpace.SMEM
HBM = pltpu.MemorySpace.HBM
GRANT = pltpu.CompilerParams(vmem_limit_bytes=16 * 2**20)


def on_chip(x):
    return pltpu.with_memory_space_constraint(x, VMEM)


def off_chip(x):
    return pltpu.with_memory_space_constraint(x, HBM)


def in_vmem(shape, dtype):
    return pltpu.VMEM(shape, dtype)


def product(refs, held, sems):
    width = held[0].shape[1]
    depth = width // CHUNKS

    def copies(k):
        at = pl.ds(k * depth, depth)
        return [
            pltpu.make_async_copy(
                ref.at[:, at] if n == 0 else ref.at[at, :],
                keep.at[:, at] if n == 0 else keep.at[at, :],
                sems.at[n, k],
            )
            for n, (ref, keep) in enumerate(zip(refs, held))
        ]

    for k in range(CHUNKS):
        for copy in copies(k):
            copy.start()
    total = None
    for k in range(CHUNKS):
        for copy in copies(k):
            copy.wait()
        at = slice(k * depth, (k + 1) * depth)
        sides = [keep[at, :] for keep in held[1:]]
        side = sides[0] if len(sides) == 1 else jnp.concatenate(sides, axis=1)
        part = jnp.dot(held[0][:, at], side, preferred_element_type=jnp.float32)
        total = part if total is None else total + part
    return total


def value_kernel(x_ref, w_ref, out_ref, x_held, w_held, sems):
    out_ref[...] = product([x_ref, w_ref], [x_held, w_held], sems).astype(out_ref.dtype)


def project_values(tokens, w_value):
    rows = tokens.shape[0]
    cols = w_value.shape[1]
    return pl.pallas_call(
        value_kernel,
        in_specs=[pl.BlockSpec(memory_space=HBM)] * 2,
        out_specs=pl.BlockSpec(memory_space=VMEM),
        out_shape=in_vmem((rows, cols), jnp.bfloat16),
        scratch_shapes=[
            pltpu.VMEM(tokens.shape, jnp.bfloat16),
            pltpu.VMEM(w_value.shape, jnp.bfloat16),
            pltpu.SemaphoreType.DMA((2, CHUNKS)),
        ],
        compiler_params=GRANT,
        name="project_values",
    )(off_chip(tokens), off_chip(w_value))


def query_key_kernel(ids_ref, x_ref, wq_ref, wk_ref, q_ref, k_ref, x_held, q_held, k_held, sems):
    rows, cols = q_ref.shape
    total = product([x_ref, wq_ref, wk_ref], [x_held, q_held, k_held], sems)
    q_ref[...] = total[:, :cols].astype(q_ref.dtype)
    k_ref[0, :rows, :] = total[:, cols:].astype(k_ref.dtype)
    row = lax.broadcasted_iota(jnp.int32, (PAD, cols), 0)
    ids = jnp.zeros((PAD, cols), jnp.float32)
    for j in range(4):
        ids = jnp.where(row == j, ids_ref[j].astype(jnp.float32), ids)
    k_ref[0, rows:, :] = ids.astype(k_ref.dtype)


def project_queries_keys(block_ids, tokens, w_query, w_key):
    rows = tokens.shape[0]
    cols = w_query.shape[1]
    return pl.pallas_call(
        query_key_kernel,
        in_specs=[pl.BlockSpec(memory_space=SMEM)] + [pl.BlockSpec(memory_space=HBM)] * 3,
        out_specs=[pl.BlockSpec(memory_space=VMEM)] * 2,
        out_shape=[
            pltpu.HBM((rows, cols), jnp.bfloat16),
            in_vmem((1, rows + PAD, cols), jnp.bfloat16),
        ],
        scratch_shapes=[
            pltpu.VMEM(tokens.shape, jnp.bfloat16),
            pltpu.VMEM(w_query.shape, jnp.bfloat16),
            pltpu.VMEM(w_key.shape, jnp.bfloat16),
            pltpu.SemaphoreType.DMA((3, CHUNKS)),
        ],
        compiler_params=GRANT,
        name="project_queries_keys",
    )(block_ids, off_chip(tokens), off_chip(w_query), off_chip(w_key))


def mix_kernel(u_ref, w_in_ref, w_out_ref, out_ref, wide_ref):
    count = u_ref.shape[1]
    hidden_units = w_in_ref.shape[0] // 2
    wide_ref[...] = u_ref[...].astype(jnp.float32)
    flat = jnp.concatenate([wide_ref[:, t, :] for t in range(count)], axis=1)
    parts = jnp.dot(w_in_ref[...], flat.astype(jnp.bfloat16), preferred_element_type=jnp.float32)
    hidden = (jax.nn.silu(parts[:hidden_units]) * parts[hidden_units:]).astype(jnp.bfloat16)
    mixed = flat + jnp.dot(w_out_ref[...], hidden, preferred_element_type=jnp.float32)
    for t in range(count):
        wide_ref[:, t, :] = mixed[:, t * HEAD_DIM : (t + 1) * HEAD_DIM]
    out_ref[...] = wide_ref[...].astype(out_ref.dtype)


def mix(gathered, w_in, w_out):
    return pl.pallas_call(
        mix_kernel,
        in_specs=[pl.BlockSpec(memory_space=VMEM)] * 3,
        out_specs=pl.BlockSpec(memory_space=VMEM),
        out_shape=in_vmem(gathered.shape, jnp.bfloat16),
        scratch_shapes=[pltpu.VMEM(gathered.shape, jnp.float32)],
        compiler_params=GRANT,
        name="mix_heads",
    )(on_chip(gathered), w_in, w_out)


def weight_kernel(ids_ref, q_ref, *refs):
    *key_refs, w_ref, total_ref, s_ref = refs
    half = q_ref.shape[0] // 2
    rows = q_ref.shape[0]
    chunk = 2 * half
    scale = HEAD_DIM ** (-0.5)
    q_row = lax.broadcasted_iota(jnp.int32, (half, 1), 0)
    lane = lax.broadcasted_iota(jnp.int32, (1, chunk), 1)
    lane_off = lane % BLK
    lane_blk = lane // BLK
    sources = [(k_ref, d) for k_ref in key_refs for d in range(k_ref.shape[0])]
    for s in range(2):
        id_lo, id_hi = ids_ref[2 * s], ids_ref[2 * s + 1]
        q_pos = jnp.where(q_row < BLK, id_lo * BLK + q_row, id_hi * BLK + q_row - BLK)
        queries = q_ref[s * half : (s + 1) * half, :]
        top = jnp.full((half, chunk), -1e30, jnp.float32)
        at = 0
        for first in range(0, len(sources), 2):
            pair = sources[first : first + 2]
            keys = jnp.concatenate(
                [k_ref[d, s * half : (s + 1) * half, :] for k_ref, d in pair], axis=0
            )
            k_ids = jnp.zeros((1, chunk), jnp.float32)
            for e, (k_ref, d) in enumerate(pair):
                tail = k_ref[d, rows:, :].astype(jnp.float32)
                for j in range(2):
                    wide = jnp.concatenate([tail[2 * s + j : 2 * s + j + 1, :]] * 3, axis=1)
                    k_ids = jnp.where(lane_blk == 2 * e + j, wide, k_ids)
            k_pos = k_ids.astype(jnp.int32) * BLK + lane_off
            scores = (
                lax.dot_general(
                    queries, keys, (((1,), (1,)), ((), ())), preferred_element_type=jnp.float32
                )
                * scale
            )
            scores = jnp.where(k_pos <= q_pos, scores, -1e30)
            s_ref[:, at : at + chunk] = scores
            top = jnp.maximum(top, scores)
            at += chunk
        top = jnp.max(top, axis=1, keepdims=True)
        total = jnp.zeros((half, chunk), jnp.float32)
        for at in range(0, s_ref.shape[1], chunk):
            weights = jnp.exp(s_ref[:, at : at + chunk] - top)
            total = total + weights
            w_ref[s, :, at : at + chunk] = weights.astype(w_ref.dtype)
        total = jnp.sum(total, axis=1, keepdims=True)
        total_ref[s * half : (s + 1) * half, :] = jnp.broadcast_to(total, (half, HEAD_DIM))


def attention_weights(block_ids, queries, keys):
    rows = queries.shape[0]
    half = rows // 2
    count = sum(piece.shape[0] for piece in keys) * half
    return pl.pallas_call(
        weight_kernel,
        in_specs=[pl.BlockSpec(memory_space=SMEM)]
        + [pl.BlockSpec(memory_space=VMEM)] * (1 + len(keys)),
        out_specs=[pl.BlockSpec(memory_space=VMEM)] * 2,
        out_shape=[
            in_vmem((2, half, count), jnp.bfloat16),
            pltpu.HBM((rows, HEAD_DIM), jnp.float32),
        ],
        scratch_shapes=[pltpu.VMEM((half, count), jnp.float32)],
        compiler_params=GRANT,
        name="attention_weights",
    )(block_ids, off_chip(queries), *keys)


def summed(spot_ref, w_ref, v_ref, s, first):
    half = w_ref.shape[1]
    sources = 4
    acc = jnp.zeros((half, HEAD_DIM), jnp.float32)
    for d in range(0, v_ref.shape[0], sources):
        values = jnp.concatenate(
            [v_ref[spot_ref[d + e], s * half : (s + 1) * half, :] for e in range(sources)], axis=0
        )
        at = first + d * half
        acc = acc + jnp.dot(
            w_ref[s, :, at : at + sources * half], values, preferred_element_type=jnp.float32
        )
    return acc


def first_kernel(spot_ref, w_ref, v_ref, part_ref):
    half = w_ref.shape[1]
    for s in range(2):
        part_ref[s * half : (s + 1) * half, :] = summed(spot_ref, w_ref, v_ref, s, 0)


def last_kernel(spot_ref, w_ref, total_ref, part_ref, v_ref, out_ref):
    half = w_ref.shape[1]
    for s in range(2):
        rows = slice(s * half, (s + 1) * half)
        acc = part_ref[rows, :] + summed(spot_ref, w_ref, v_ref, s, w_ref.shape[2] // 2)
        out_ref[rows, :] = (acc / total_ref[rows, :]).astype(out_ref.dtype)


def apply_first(spots, weights, values):
    rows = values.shape[1]
    return pl.pallas_call(
        first_kernel,
        in_specs=[pl.BlockSpec(memory_space=SMEM)] + [pl.BlockSpec(memory_space=VMEM)] * 2,
        out_specs=pl.BlockSpec(memory_space=VMEM),
        out_shape=in_vmem((rows, HEAD_DIM), jnp.float32),
        compiler_params=GRANT,
        name="apply_first",
    )(spots, weights, on_chip(values))


def apply_last(spots, weights, total, part, values):
    return pl.pallas_call(
        last_kernel,
        in_specs=[pl.BlockSpec(memory_space=SMEM)] + [pl.BlockSpec(memory_space=VMEM)] * 4,
        out_specs=pl.BlockSpec(memory_space=VMEM),
        out_shape=jax.ShapeDtypeStruct(total.shape, jnp.bfloat16),
        compiler_params=GRANT,
        name="apply_last",
    )(spots, weights, off_chip(total), part, on_chip(values))


def pack_kernel(*refs):
    *pieces, out_ref = refs
    for n in range(out_ref.shape[0]):
        out_ref[n] = pieces[n % len(pieces)][0]


def pack(count, *pieces):
    return pl.pallas_call(
        pack_kernel,
        in_specs=[pl.BlockSpec(memory_space=VMEM)] * len(pieces),
        out_specs=pl.BlockSpec(memory_space=VMEM),
        out_shape=in_vmem((count, *pieces[0].shape[1:]), pieces[0].dtype),
        compiler_params=GRANT,
        name="pack",
    )(*[on_chip(piece) for piece in pieces])


def shards(tokens, w_query, w_key, w_value, mix_gate, mix_up, mix_down, block_ids):
    heads = mix_gate.shape[0]
    rows = tokens.shape[0]

    def exchange(x):
        return lax.all_to_all(x, "tensor", split_axis=0, concat_axis=0, tiled=True)

    def spread(x):
        return lax.all_to_all(
            x, "context", split_axis=0, concat_axis=0, axis_index_groups=CORE_GROUPS, tiled=True
        )

    def flip(x, bit):
        return lax.ppermute(x, "context", [(i, i ^ bit) for i in range(16)])

    w_in = jnp.concatenate([mix_gate, mix_up], axis=1).T
    w_out = mix_down.T
    values = project_values(tokens, w_value)
    gathered = exchange(values.reshape(heads, rows // heads, HEAD_DIM))
    tokens, values = lax.optimization_barrier((tokens, values))
    queries, own = project_queries_keys(block_ids, tokens, w_query, w_key)
    beside = flip(own, 2)
    far = flip(own, 8)
    mixed = mix(gathered, w_in, w_out)
    mixed_rows = exchange(mixed).reshape(1, rows, HEAD_DIM)
    far_beside = flip(far, 2)
    quad = pack(4, own, beside, far, far_beside)
    near = flip(quad, 4)
    keys = [quad, near, flip(quad, 1), flip(near, 1)]
    turn = jnp.arange(8, dtype=jnp.int32)
    spots = (lax.axis_index("context") // 2) ^ (turn % 2 + turn // 2 % 2 * 4 + turn // 4 * 2)
    weights, total = attention_weights(block_ids, queries, keys)
    copies = pack(8, mixed_rows)
    values_mine = spread(copies)
    values_other = flip(values_mine, 1)
    part = apply_first(spots, weights, values_mine)
    return apply_last(spots, weights, total, part, values_other)


def solution(mesh):
    in_specs = (
        P("context", None),
        P(None, "tensor"),
        P(None, "tensor"),
        P(None, "tensor"),
        P(),
        P(),
        P(),
        P("context"),
    )
    out_specs = P("context", "tensor")
    return jax.shard_map(shards, mesh=mesh, in_specs=in_specs, out_specs=out_specs, check_vma=False)
```

```python
import jax
import jax.numpy as jnp
from jax import lax
from jax.experimental import pallas as pl
from jax.experimental.pallas import tpu as pltpu
from jax.sharding import PartitionSpec as P


HEAD_DIM = 128
BLK = 96
PAD = 16
CHUNKS = 8
CORE_GROUPS = [[2 * k + core for k in range(8)] for core in range(2)]
VMEM = pltpu.MemorySpace.VMEM
SMEM = pltpu.MemorySpace.SMEM
HBM = pltpu.MemorySpace.HBM
GRANT = pltpu.CompilerParams(vmem_limit_bytes=16 * 2**20)


def on_chip(x):
    return pltpu.with_memory_space_constraint(x, VMEM)


def off_chip(x):
    return pltpu.with_memory_space_constraint(x, HBM)


def in_vmem(shape, dtype):
    return pltpu.VMEM(shape, dtype)


def product(refs, held, sems):
    rows, width = held[0].shape
    depth = width // CHUNKS
    third = rows // 3

    def copies(k):
        at = pl.ds(k * depth, depth)
        return [
            pltpu.make_async_copy(
                ref.at[:, at] if n == 0 else ref.at[at, :],
                keep.at[:, at] if n == 0 else keep.at[at, :],
                sems.at[n, k],
            )
            for n, (ref, keep) in enumerate(zip(refs, held))
        ]

    for k in range(CHUNKS):
        for copy in copies(k):
            copy.start()
    totals = [None] * 3
    for k in range(CHUNKS):
        for copy in copies(k):
            copy.wait()
        at = slice(k * depth, (k + 1) * depth)
        sides = [keep[at, :] for keep in held[1:]]
        side = sides[0] if len(sides) == 1 else jnp.concatenate(sides, axis=1)
        for n in range(3):
            part = jnp.dot(
                held[0][n * third : (n + 1) * third, at], side, preferred_element_type=jnp.float32
            )
            totals[n] = part if totals[n] is None else totals[n] + part
    return jnp.concatenate(totals, axis=0)


def value_kernel(x_ref, w_ref, out_ref, x_held, w_held, sems):
    out_ref[...] = product([x_ref, w_ref], [x_held, w_held], sems).astype(out_ref.dtype)


def project_values(tokens, w_value):
    rows = tokens.shape[0]
    cols = w_value.shape[1]
    return pl.pallas_call(
        value_kernel,
        in_specs=[pl.BlockSpec(memory_space=HBM)] * 2,
        out_specs=pl.BlockSpec(memory_space=VMEM),
        out_shape=in_vmem((rows, cols), jnp.bfloat16),
        scratch_shapes=[
            pltpu.VMEM(tokens.shape, jnp.bfloat16),
            pltpu.VMEM(w_value.shape, jnp.bfloat16),
            pltpu.SemaphoreType.DMA((2, CHUNKS)),
        ],
        compiler_params=GRANT,
        name="project_values",
    )(off_chip(tokens), off_chip(w_value))


def query_key_kernel(ids_ref, x_ref, wq_ref, wk_ref, q_ref, k_ref, x_held, q_held, k_held, sems):
    rows, cols = q_ref.shape
    total = product([x_ref, wq_ref, wk_ref], [x_held, q_held, k_held], sems)
    q_ref[...] = total[:, :cols].astype(q_ref.dtype)
    k_ref[0, :rows, :] = total[:, cols:].astype(k_ref.dtype)
    row = lax.broadcasted_iota(jnp.int32, (PAD, cols), 0)
    ids = jnp.zeros((PAD, cols), jnp.float32)
    for j in range(4):
        ids = jnp.where(row == j, ids_ref[j].astype(jnp.float32), ids)
    k_ref[0, rows:, :] = ids.astype(k_ref.dtype)


def project_queries_keys(block_ids, tokens, w_query, w_key):
    rows = tokens.shape[0]
    cols = w_query.shape[1]
    return pl.pallas_call(
        query_key_kernel,
        in_specs=[pl.BlockSpec(memory_space=SMEM)] + [pl.BlockSpec(memory_space=HBM)] * 3,
        out_specs=[pl.BlockSpec(memory_space=VMEM)] * 2,
        out_shape=[
            pltpu.HBM((rows, cols), jnp.bfloat16),
            in_vmem((1, rows + PAD, cols), jnp.bfloat16),
        ],
        scratch_shapes=[
            pltpu.VMEM(tokens.shape, jnp.bfloat16),
            pltpu.VMEM(w_query.shape, jnp.bfloat16),
            pltpu.VMEM(w_key.shape, jnp.bfloat16),
            pltpu.SemaphoreType.DMA((3, CHUNKS)),
        ],
        compiler_params=GRANT,
        name="project_queries_keys",
    )(off_chip(block_ids), off_chip(tokens), off_chip(w_query), off_chip(w_key))


def mix_kernel(u_ref, w_in_ref, w_out_ref, out_ref, wide_ref):
    count = u_ref.shape[1]
    hidden_units = w_in_ref.shape[0] // 2
    wide_ref[...] = u_ref[...].astype(jnp.float32)
    flat = jnp.concatenate([wide_ref[:, t, :] for t in range(count)], axis=1)
    parts = jnp.dot(w_in_ref[...], flat.astype(jnp.bfloat16), preferred_element_type=jnp.float32)
    hidden = (jax.nn.silu(parts[:hidden_units]) * parts[hidden_units:]).astype(jnp.bfloat16)
    mixed = flat + jnp.dot(w_out_ref[...], hidden, preferred_element_type=jnp.float32)
    for t in range(count):
        wide_ref[:, t, :] = mixed[:, t * HEAD_DIM : (t + 1) * HEAD_DIM]
    out_ref[...] = wide_ref[...].astype(out_ref.dtype)


def mix(gathered, w_in, w_out):
    return pl.pallas_call(
        mix_kernel,
        in_specs=[pl.BlockSpec(memory_space=VMEM)] * 3,
        out_specs=pl.BlockSpec(memory_space=VMEM),
        out_shape=in_vmem(gathered.shape, jnp.bfloat16),
        scratch_shapes=[pltpu.VMEM(gathered.shape, jnp.float32)],
        compiler_params=GRANT,
        name="mix_heads",
    )(on_chip(gathered), w_in, w_out)


def weight_kernel(ids_ref, q_ref, *refs):
    quad_ref, near_ref, far_quad_ref, far_near_ref, w_ref, total_ref, s_ref, *held, sems = refs
    copies = [
        pltpu.make_async_copy(ref, keep, sems.at[n])
        for n, (ref, keep) in enumerate(zip((near_ref, far_quad_ref), held))
    ]
    for copy in copies:
        copy.start()
    key_refs = [quad_ref, *held, far_near_ref]
    half = q_ref.shape[0] // 2
    rows = q_ref.shape[0]
    chunk = 2 * half
    scale = HEAD_DIM ** (-0.5)
    q_row = lax.broadcasted_iota(jnp.int32, (half, 1), 0)
    lane = lax.broadcasted_iota(jnp.int32, (1, chunk), 1)
    lane_off = lane % BLK
    lane_blk = lane // BLK
    sources = [(k_ref, d) for k_ref in key_refs for d in range(k_ref.shape[0])]
    for s in range(2):
        id_lo, id_hi = ids_ref[2 * s], ids_ref[2 * s + 1]
        q_pos = jnp.where(q_row < BLK, id_lo * BLK + q_row, id_hi * BLK + q_row - BLK)
        queries = q_ref[s * half : (s + 1) * half, :]
        top = jnp.full((half, chunk), -1e30, jnp.float32)
        at = 0
        for first in range(0, len(sources), 2):
            pair = sources[first : first + 2]
            if s == 0 and first in (4, 8):
                copies[first // 4 - 1].wait()
            keys = jnp.concatenate(
                [k_ref[d, s * half : (s + 1) * half, :] for k_ref, d in pair], axis=0
            )
            k_ids = jnp.zeros((1, chunk), jnp.float32)
            for e, (k_ref, d) in enumerate(pair):
                tail = k_ref[d, rows:, :].astype(jnp.float32)
                for j in range(2):
                    wide = jnp.concatenate([tail[2 * s + j : 2 * s + j + 1, :]] * 3, axis=1)
                    k_ids = jnp.where(lane_blk == 2 * e + j, wide, k_ids)
            k_pos = k_ids.astype(jnp.int32) * BLK + lane_off
            scores = (
                lax.dot_general(
                    queries, keys, (((1,), (1,)), ((), ())), preferred_element_type=jnp.float32
                )
                * scale
            )
            scores = jnp.where(k_pos <= q_pos, scores, -1e30)
            s_ref[:, at : at + chunk] = scores
            top = jnp.maximum(top, scores)
            at += chunk
        top = jnp.max(top, axis=1, keepdims=True)
        total = jnp.zeros((half, chunk), jnp.float32)
        for at in range(0, s_ref.shape[1], chunk):
            weights = jnp.exp(s_ref[:, at : at + chunk] - top)
            total = total + weights
            w_ref[s, :, at : at + chunk] = weights.astype(w_ref.dtype)
        total = jnp.sum(total, axis=1, keepdims=True)
        total_ref[s * half : (s + 1) * half, :] = jnp.broadcast_to(total, (half, HEAD_DIM))


def attention_weights(block_ids, queries, keys):
    rows = queries.shape[0]
    half = rows // 2
    count = sum(piece.shape[0] for piece in keys) * half
    places = [on_chip, off_chip, off_chip, on_chip]
    return pl.pallas_call(
        weight_kernel,
        in_specs=[pl.BlockSpec(memory_space=SMEM)]
        + [pl.BlockSpec(memory_space=space) for space in (VMEM, VMEM, HBM, HBM, VMEM)],
        out_specs=[pl.BlockSpec(memory_space=VMEM)] * 2,
        out_shape=[
            in_vmem((2, half, count), jnp.bfloat16),
            pltpu.HBM((rows, HEAD_DIM), jnp.float32),
        ],
        scratch_shapes=[
            pltpu.VMEM((half, count), jnp.float32),
            pltpu.VMEM(keys[1].shape, jnp.bfloat16),
            pltpu.VMEM(keys[2].shape, jnp.bfloat16),
            pltpu.SemaphoreType.DMA((2,)),
        ],
        compiler_params=GRANT,
        name="attention_weights",
    )(off_chip(block_ids), off_chip(queries), *[place(k) for place, k in zip(places, keys)])


def summed(w_ref, v_ref, s, first):
    half = w_ref.shape[1]
    sources = 4
    mine = lax.axis_index("context") // 2
    acc = jnp.zeros((half, HEAD_DIM), jnp.float32)
    for d in range(0, v_ref.shape[0], sources):
        turns = [e % 2 + e // 2 % 2 * 4 + e // 4 * 2 for e in range(d, d + sources)]
        values = jnp.concatenate(
            [v_ref[mine ^ turn, s * half : (s + 1) * half, :] for turn in turns], axis=0
        )
        at = first + d * half
        acc = acc + jnp.dot(
            w_ref[s, :, at : at + sources * half], values, preferred_element_type=jnp.float32
        )
    return acc


def first_kernel(w_ref, total_ref, v_ref, part_ref, kept_ref):
    half = w_ref.shape[1]
    for s in range(2):
        part_ref[s * half : (s + 1) * half, :] = summed(w_ref, v_ref, s, 0)
    kept_ref[...] = total_ref[...]


def last_kernel(w_ref, total_ref, part_ref, v_ref, out_ref):
    half = w_ref.shape[1]
    for s in range(2):
        rows = slice(s * half, (s + 1) * half)
        acc = part_ref[rows, :] + summed(w_ref, v_ref, s, w_ref.shape[2] // 2)
        out_ref[rows, :] = (acc / total_ref[rows, :]).astype(out_ref.dtype)


def apply_first(weights, total, values):
    return pl.pallas_call(
        first_kernel,
        in_specs=[pl.BlockSpec(memory_space=VMEM)] * 3,
        out_specs=[pl.BlockSpec(memory_space=VMEM)] * 2,
        out_shape=[in_vmem(total.shape, jnp.float32)] * 2,
        compiler_params=GRANT,
        name="apply_first",
    )(weights, off_chip(total), on_chip(values))


def apply_last(weights, total, part, values):
    return pl.pallas_call(
        last_kernel,
        in_specs=[pl.BlockSpec(memory_space=VMEM)] * 4,
        out_specs=pl.BlockSpec(memory_space=VMEM),
        out_shape=jax.ShapeDtypeStruct(total.shape, jnp.bfloat16),
        compiler_params=GRANT,
        name="apply_last",
    )(weights, total, part, on_chip(values))


def pack_kernel(*refs):
    *pieces, out_ref = refs
    for n, piece in enumerate(pieces):
        out_ref[n] = piece[0]


def pack(*pieces):
    return pl.pallas_call(
        pack_kernel,
        in_specs=[pl.BlockSpec(memory_space=VMEM)] * len(pieces),
        out_specs=pl.BlockSpec(memory_space=VMEM),
        out_shape=in_vmem((len(pieces), *pieces[0].shape[1:]), pieces[0].dtype),
        compiler_params=GRANT,
        name="pack",
    )(*[on_chip(piece) for piece in pieces])


def repeat_kernel(x_ref, out_ref, sems):
    copies = [
        pltpu.make_async_copy(x_ref, out_ref.at[n], sems.at[n]) for n in range(out_ref.shape[0])
    ]
    for copy in copies:
        copy.start()
    for copy in copies:
        copy.wait()


def repeat(x, count):
    return pl.pallas_call(
        repeat_kernel,
        in_specs=[pl.BlockSpec(memory_space=VMEM)],
        out_specs=pl.BlockSpec(memory_space=HBM),
        out_shape=pltpu.HBM((count, *x.shape), x.dtype),
        scratch_shapes=[pltpu.SemaphoreType.DMA((count,))],
        compiler_params=GRANT,
        name="repeat",
    )(on_chip(x))


def shards(tokens, w_query, w_key, w_value, mix_gate, mix_up, mix_down, block_ids):
    heads = mix_gate.shape[0]
    rows = tokens.shape[0]

    def exchange(x):
        return lax.all_to_all(x, "tensor", split_axis=0, concat_axis=0, tiled=True)

    def spread(x):
        return lax.all_to_all(
            x, "context", split_axis=0, concat_axis=0, axis_index_groups=CORE_GROUPS, tiled=True
        )

    def flip(x, bit):
        return lax.ppermute(x, "context", [(i, i ^ bit) for i in range(16)])

    w_in = jnp.concatenate([mix_gate, mix_up], axis=1).T
    w_out = mix_down.T
    values = project_values(tokens, w_value)
    gathered = exchange(values.reshape(heads, rows // heads, HEAD_DIM))
    tokens, values = lax.optimization_barrier((tokens, values))
    queries, own = project_queries_keys(block_ids, tokens, w_query, w_key)
    beside = flip(own, 2)
    far = flip(own, 8)
    mixed = mix(gathered, w_in, w_out)
    mixed_rows = exchange(mixed).reshape(rows, HEAD_DIM)
    far_beside = flip(far, 2)
    quad = pack(own, beside, far, far_beside)
    near = flip(quad, 4)
    other_quad = flip(quad, 1)
    other_near = flip(near, 1)
    keys = [quad, near, other_quad, other_near]
    weights, total = attention_weights(block_ids, queries, keys)
    copies = repeat(mixed_rows, 8)
    values_mine = spread(copies)
    values_other = flip(values_mine, 1)
    part, total = apply_first(weights, total, values_mine)
    return apply_last(weights, total, part, values_other)


def solution(mesh):
    in_specs = (
        P("context", None),
        P(None, "tensor"),
        P(None, "tensor"),
        P(None, "tensor"),
        P(),
        P(),
        P(),
        P("context"),
    )
    out_specs = P("context", "tensor")
    return jax.shard_map(shards, mesh=mesh, in_specs=in_specs, out_specs=out_specs, check_vma=False)
```

```python
import jax
import jax.numpy as jnp
from jax import lax
from jax.experimental import pallas as pl
from jax.experimental.pallas import tpu as pltpu
from jax.sharding import PartitionSpec as P


HEAD_DIM = 128
BLK = 96
PAD = 16
CHUNKS = 8
STEPS = (0, 3, 1, 2)
CORE_GROUPS = [[2 * k + core for k in range(8)] for core in range(2)]
VMEM = pltpu.MemorySpace.VMEM
SMEM = pltpu.MemorySpace.SMEM
HBM = pltpu.MemorySpace.HBM
GRANT = pltpu.CompilerParams(vmem_limit_bytes=16 * 2**20)


def on_chip(x):
    return pltpu.with_memory_space_constraint(x, VMEM)


def off_chip(x):
    return pltpu.with_memory_space_constraint(x, HBM)


def in_vmem(shape, dtype):
    return pltpu.VMEM(shape, dtype)


def product(refs, held, sems):
    rows, width = held[0].shape
    depth = width // CHUNKS
    third = rows // 3

    def copies(k):
        at = pl.ds(k * depth, depth)
        return [
            pltpu.make_async_copy(
                ref.at[:, at] if n == 0 else ref.at[at, :],
                keep.at[:, at] if n == 0 else keep.at[at, :],
                sems.at[n, k],
            )
            for n, (ref, keep) in enumerate(zip(refs, held))
        ]

    for k in range(CHUNKS):
        for copy in copies(k):
            copy.start()
    totals = [None] * 3
    for k in range(CHUNKS):
        for copy in copies(k):
            copy.wait()
        at = slice(k * depth, (k + 1) * depth)
        sides = [keep[at, :] for keep in held[1:]]
        side = sides[0] if len(sides) == 1 else jnp.concatenate(sides, axis=1)
        for n in range(3):
            part = jnp.dot(
                held[0][n * third : (n + 1) * third, at], side, preferred_element_type=jnp.float32
            )
            totals[n] = part if totals[n] is None else totals[n] + part
    return jnp.concatenate(totals, axis=0)


def value_kernel(x_ref, w_ref, out_ref, x_held, w_held, sems):
    out_ref[...] = product([x_ref, w_ref], [x_held, w_held], sems).astype(out_ref.dtype)


def project_values(tokens, w_value):
    rows = tokens.shape[0]
    cols = w_value.shape[1]
    return pl.pallas_call(
        value_kernel,
        in_specs=[pl.BlockSpec(memory_space=HBM)] * 2,
        out_specs=pl.BlockSpec(memory_space=VMEM),
        out_shape=in_vmem((rows, cols), jnp.bfloat16),
        scratch_shapes=[
            pltpu.VMEM(tokens.shape, jnp.bfloat16),
            pltpu.VMEM(w_value.shape, jnp.bfloat16),
            pltpu.SemaphoreType.DMA((2, CHUNKS)),
        ],
        compiler_params=GRANT,
        name="project_values",
    )(off_chip(tokens), off_chip(w_value))


def query_key_kernel(ids_ref, x_ref, wq_ref, wk_ref, q_ref, k_ref, x_held, q_held, k_held, sems):
    rows, cols = q_ref.shape
    total = product([x_ref, wq_ref, wk_ref], [x_held, q_held, k_held], sems)
    q_ref[...] = total[:, :cols].astype(q_ref.dtype)
    k_ref[0, :rows, :] = total[:, cols:].astype(k_ref.dtype)
    row = lax.broadcasted_iota(jnp.int32, (PAD, cols), 0)
    ids = jnp.zeros((PAD, cols), jnp.float32)
    for j in range(4):
        ids = jnp.where(row == j, ids_ref[j].astype(jnp.float32), ids)
    k_ref[0, rows:, :] = ids.astype(k_ref.dtype)


def project_queries_keys(block_ids, tokens, w_query, w_key):
    rows = tokens.shape[0]
    cols = w_query.shape[1]
    return pl.pallas_call(
        query_key_kernel,
        in_specs=[pl.BlockSpec(memory_space=SMEM)] + [pl.BlockSpec(memory_space=HBM)] * 3,
        out_specs=[pl.BlockSpec(memory_space=VMEM)] * 2,
        out_shape=[
            pltpu.HBM((rows, cols), jnp.bfloat16),
            in_vmem((1, rows + PAD, cols), jnp.bfloat16),
        ],
        scratch_shapes=[
            pltpu.VMEM(tokens.shape, jnp.bfloat16),
            pltpu.VMEM(w_query.shape, jnp.bfloat16),
            pltpu.VMEM(w_key.shape, jnp.bfloat16),
            pltpu.SemaphoreType.DMA((3, CHUNKS)),
        ],
        compiler_params=GRANT,
        name="project_queries_keys",
    )(off_chip(block_ids), off_chip(tokens), off_chip(w_query), off_chip(w_key))


def mix_kernel(u_ref, w_in_ref, w_out_ref, out_ref, wide_ref):
    count = u_ref.shape[1]
    hidden_units = w_in_ref.shape[0] // 2
    wide_ref[...] = u_ref[...].astype(jnp.float32)
    flat = jnp.concatenate([wide_ref[:, t, :] for t in range(count)], axis=1)
    parts = jnp.dot(w_in_ref[...], flat.astype(jnp.bfloat16), preferred_element_type=jnp.float32)
    hidden = (jax.nn.silu(parts[:hidden_units]) * parts[hidden_units:]).astype(jnp.bfloat16)
    mixed = flat + jnp.dot(w_out_ref[...], hidden, preferred_element_type=jnp.float32)
    for t in range(count):
        wide_ref[:, t, :] = mixed[:, t * HEAD_DIM : (t + 1) * HEAD_DIM]
    out_ref[...] = wide_ref[...].astype(out_ref.dtype)


def mix(gathered, w_in, w_out):
    return pl.pallas_call(
        mix_kernel,
        in_specs=[pl.BlockSpec(memory_space=VMEM)] * 3,
        out_specs=pl.BlockSpec(memory_space=VMEM),
        out_shape=in_vmem(gathered.shape, jnp.bfloat16),
        scratch_shapes=[pltpu.VMEM(gathered.shape, jnp.float32)],
        compiler_params=GRANT,
        name="mix_heads",
    )(on_chip(gathered), w_in, w_out)


def weight_kernel(ids_ref, q_ref, *refs):
    *key_refs, w_ref, total_ref, s_ref = refs
    half = q_ref.shape[0] // 2
    rows = q_ref.shape[0]
    chunk = 2 * half
    scale = HEAD_DIM ** (-0.5)
    q_row = lax.broadcasted_iota(jnp.int32, (half, 1), 0)
    lane = lax.broadcasted_iota(jnp.int32, (1, chunk), 1)
    lane_off = lane % BLK
    lane_blk = lane // BLK
    sources = [(k_ref, d) for k_ref in key_refs for d in range(k_ref.shape[0])]
    for s in range(2):
        id_lo, id_hi = ids_ref[2 * s], ids_ref[2 * s + 1]
        q_pos = jnp.where(q_row < BLK, id_lo * BLK + q_row, id_hi * BLK + q_row - BLK)
        queries = q_ref[s * half : (s + 1) * half, :]
        top = jnp.full((half, chunk), -1e30, jnp.float32)
        at = 0
        for first in range(0, len(sources), 2):
            pair = sources[first : first + 2]
            keys = jnp.concatenate(
                [k_ref[d, s * half : (s + 1) * half, :] for k_ref, d in pair], axis=0
            )
            k_ids = jnp.zeros((1, chunk), jnp.float32)
            for e, (k_ref, d) in enumerate(pair):
                tail = k_ref[d, rows:, :].astype(jnp.float32)
                for j in range(2):
                    wide = jnp.concatenate([tail[2 * s + j : 2 * s + j + 1, :]] * 3, axis=1)
                    k_ids = jnp.where(lane_blk == 2 * e + j, wide, k_ids)
            k_pos = k_ids.astype(jnp.int32) * BLK + lane_off
            scores = (
                lax.dot_general(
                    queries, keys, (((1,), (1,)), ((), ())), preferred_element_type=jnp.float32
                )
                * scale
            )
            scores = jnp.where(k_pos <= q_pos, scores, -1e30)
            s_ref[:, at : at + chunk] = scores
            top = jnp.maximum(top, scores)
            at += chunk
        top = jnp.max(top, axis=1, keepdims=True)
        total = jnp.zeros((half, chunk), jnp.float32)
        for at in range(0, s_ref.shape[1], chunk):
            weights = jnp.exp(s_ref[:, at : at + chunk] - top)
            total = total + weights
            w_ref[s, :, at : at + chunk] = weights.astype(w_ref.dtype)
        total = jnp.sum(total, axis=1, keepdims=True)
        total_ref[s * half : (s + 1) * half, :] = jnp.broadcast_to(total, (half, HEAD_DIM))


def attention_weights(block_ids, queries, keys):
    rows = queries.shape[0]
    half = rows // 2
    count = sum(piece.shape[0] for piece in keys) * half
    return pl.pallas_call(
        weight_kernel,
        in_specs=[pl.BlockSpec(memory_space=SMEM)]
        + [pl.BlockSpec(memory_space=VMEM)] * (1 + len(keys)),
        out_specs=[pl.BlockSpec(memory_space=VMEM)] * 2,
        out_shape=[
            in_vmem((2, half, count), jnp.bfloat16),
            pltpu.HBM((rows, HEAD_DIM), jnp.float32),
        ],
        scratch_shapes=[pltpu.VMEM((half, count), jnp.float32)],
        compiler_params=GRANT,
        name="attention_weights",
    )(off_chip(block_ids), off_chip(queries), *[on_chip(k) for k in keys])


def summed(w_ref, v_ref, s, first):
    half = w_ref.shape[1]
    sources = 4
    mine = lax.axis_index("context") // 2
    acc = jnp.zeros((half, HEAD_DIM), jnp.float32)
    for d in range(0, v_ref.shape[0], sources):
        spots = [((mine + 2 * STEPS[e // 2]) & 7) ^ (e % 2) for e in range(d, d + sources)]
        values = jnp.concatenate(
            [v_ref[spot, s * half : (s + 1) * half, :] for spot in spots], axis=0
        )
        at = first + d * half
        acc = acc + jnp.dot(
            w_ref[s, :, at : at + sources * half], values, preferred_element_type=jnp.float32
        )
    return acc


def first_kernel(w_ref, total_ref, v_ref, part_ref, kept_ref):
    half = w_ref.shape[1]
    for s in range(2):
        part_ref[s * half : (s + 1) * half, :] = summed(w_ref, v_ref, s, 0)
    kept_ref[...] = total_ref[...]


def last_kernel(w_ref, total_ref, part_ref, v_ref, out_ref):
    half = w_ref.shape[1]
    for s in range(2):
        rows = slice(s * half, (s + 1) * half)
        acc = part_ref[rows, :] + summed(w_ref, v_ref, s, w_ref.shape[2] // 2)
        out_ref[rows, :] = (acc / total_ref[rows, :]).astype(out_ref.dtype)


def apply_first(weights, total, values):
    return pl.pallas_call(
        first_kernel,
        in_specs=[pl.BlockSpec(memory_space=VMEM)] * 3,
        out_specs=[pl.BlockSpec(memory_space=VMEM)] * 2,
        out_shape=[in_vmem(total.shape, jnp.float32)] * 2,
        compiler_params=GRANT,
        name="apply_first",
    )(weights, off_chip(total), on_chip(values))


def apply_last(weights, total, part, values):
    return pl.pallas_call(
        last_kernel,
        in_specs=[pl.BlockSpec(memory_space=VMEM)] * 4,
        out_specs=pl.BlockSpec(memory_space=VMEM),
        out_shape=jax.ShapeDtypeStruct(total.shape, jnp.bfloat16),
        compiler_params=GRANT,
        name="apply_last",
    )(weights, total, part, on_chip(values))


def pack_kernel(*refs):
    *pieces, out_ref = refs
    n = 0
    for piece in pieces:
        out_ref[n : n + piece.shape[0]] = piece[...]
        n += piece.shape[0]


def pack(*pieces):
    count = sum(piece.shape[0] for piece in pieces)
    return pl.pallas_call(
        pack_kernel,
        in_specs=[pl.BlockSpec(memory_space=VMEM)] * len(pieces),
        out_specs=pl.BlockSpec(memory_space=VMEM),
        out_shape=in_vmem((count, *pieces[0].shape[1:]), pieces[0].dtype),
        compiler_params=GRANT,
        name="pack",
    )(*[on_chip(piece) for piece in pieces])


def repeat_kernel(x_ref, out_ref, sems):
    copies = [
        pltpu.make_async_copy(x_ref, out_ref.at[n], sems.at[n]) for n in range(out_ref.shape[0])
    ]
    for copy in copies:
        copy.start()
    for copy in copies:
        copy.wait()


def repeat(x, count):
    return pl.pallas_call(
        repeat_kernel,
        in_specs=[pl.BlockSpec(memory_space=VMEM)],
        out_specs=pl.BlockSpec(memory_space=HBM),
        out_shape=pltpu.HBM((count, *x.shape), x.dtype),
        scratch_shapes=[pltpu.SemaphoreType.DMA((count,))],
        compiler_params=GRANT,
        name="repeat",
    )(on_chip(x))


def shards(tokens, w_query, w_key, w_value, mix_gate, mix_up, mix_down, block_ids):
    heads = mix_gate.shape[0]
    rows = tokens.shape[0]

    def exchange(x):
        return lax.all_to_all(x, "tensor", split_axis=0, concat_axis=0, tiled=True)

    def spread(x):
        return lax.all_to_all(
            x, "context", split_axis=0, concat_axis=0, axis_index_groups=CORE_GROUPS, tiled=True
        )

    def flip(x, bit):
        return lax.ppermute(x, "context", [(i, i ^ bit) for i in range(16)])

    def along(x, step):
        return lax.ppermute(x, "context", [(i, (i + 4 * step) % 16) for i in range(16)])

    w_in = jnp.concatenate([mix_gate, mix_up], axis=1).T
    w_out = mix_down.T
    values = project_values(tokens, w_value)
    gathered = exchange(values.reshape(heads, rows // heads, HEAD_DIM))
    tokens, values = lax.optimization_barrier((tokens, values))
    queries, own = project_queries_keys(block_ids, tokens, w_query, w_key)
    beside = flip(own, 2)
    mixed = mix(gathered, w_in, w_out)
    mixed_rows = exchange(mixed).reshape(rows, HEAD_DIM)
    pair = pack(own, beside)
    up = along(pair, 1)
    down = along(pair, 3)
    far = along(pair, 2)
    keys = pack(pair, up, down, far)
    other_keys = flip(keys, 1)
    weights, total = attention_weights(block_ids, queries, [keys, other_keys])
    copies = repeat(mixed_rows, 8)
    values_mine = spread(copies)
    values_other = flip(values_mine, 1)
    part, total = apply_first(weights, total, values_mine)
    return apply_last(weights, total, part, values_other)


def solution(mesh):
    in_specs = (
        P("context", None),
        P(None, "tensor"),
        P(None, "tensor"),
        P(None, "tensor"),
        P(),
        P(),
        P(),
        P("context"),
    )
    out_specs = P("context", "tensor")
    return jax.shard_map(shards, mesh=mesh, in_specs=in_specs, out_specs=out_specs, check_vma=False)
```

```python
import jax
import jax.numpy as jnp
from jax import lax
from jax.experimental import pallas as pl
from jax.experimental.pallas import tpu as pltpu
from jax.sharding import PartitionSpec as P


HEAD_DIM = 128
BLK = 96
PAD = 16
CHUNKS = 8
STEPS = (0, 1, 3, 2)
CORE_GROUPS = [[2 * k + core for k in range(8)] for core in range(2)]
VMEM = pltpu.MemorySpace.VMEM
SMEM = pltpu.MemorySpace.SMEM
HBM = pltpu.MemorySpace.HBM
GRANT = pltpu.CompilerParams(vmem_limit_bytes=16 * 2**20)


def on_chip(x):
    return pltpu.with_memory_space_constraint(x, VMEM)


def off_chip(x):
    return pltpu.with_memory_space_constraint(x, HBM)


def in_vmem(shape, dtype):
    return pltpu.VMEM(shape, dtype)


def product(refs, held, sems):
    rows, width = held[0].shape
    depth = width // CHUNKS
    third = rows // 3

    def copies(k):
        at = pl.ds(k * depth, depth)
        return [
            pltpu.make_async_copy(
                ref.at[:, at] if n == 0 else ref.at[at, :],
                keep.at[:, at] if n == 0 else keep.at[at, :],
                sems.at[n, k],
            )
            for n, (ref, keep) in enumerate(zip(refs, held))
        ]

    for k in range(CHUNKS):
        for copy in copies(k):
            copy.start()
    totals = [None] * 3
    for k in range(CHUNKS):
        for copy in copies(k):
            copy.wait()
        at = slice(k * depth, (k + 1) * depth)
        sides = [keep[at, :] for keep in held[1:]]
        side = sides[0] if len(sides) == 1 else jnp.concatenate(sides, axis=1)
        for n in range(3):
            part = jnp.dot(
                held[0][n * third : (n + 1) * third, at], side, preferred_element_type=jnp.float32
            )
            totals[n] = part if totals[n] is None else totals[n] + part
    return jnp.concatenate(totals, axis=0)


def value_kernel(x_ref, w_ref, out_ref, x_held, w_held, sems):
    out_ref[...] = product([x_ref, w_ref], [x_held, w_held], sems).astype(out_ref.dtype)


def project_values(tokens, w_value):
    rows = tokens.shape[0]
    cols = w_value.shape[1]
    return pl.pallas_call(
        value_kernel,
        in_specs=[pl.BlockSpec(memory_space=HBM)] * 2,
        out_specs=pl.BlockSpec(memory_space=VMEM),
        out_shape=in_vmem((rows, cols), jnp.bfloat16),
        scratch_shapes=[
            pltpu.VMEM(tokens.shape, jnp.bfloat16),
            pltpu.VMEM(w_value.shape, jnp.bfloat16),
            pltpu.SemaphoreType.DMA((2, CHUNKS)),
        ],
        compiler_params=GRANT,
        name="project_values",
    )(off_chip(tokens), off_chip(w_value))


def query_key_kernel(ids_ref, x_ref, wq_ref, wk_ref, q_ref, k_ref, x_held, q_held, k_held, sems):
    rows, cols = q_ref.shape
    total = product([x_ref, wq_ref, wk_ref], [x_held, q_held, k_held], sems)
    q_ref[...] = total[:, :cols].astype(q_ref.dtype)
    k_ref[0, :rows, :] = total[:, cols:].astype(k_ref.dtype)
    row = lax.broadcasted_iota(jnp.int32, (PAD, cols), 0)
    ids = jnp.zeros((PAD, cols), jnp.float32)
    for j in range(4):
        ids = jnp.where(row == j, ids_ref[j].astype(jnp.float32), ids)
    k_ref[0, rows:, :] = ids.astype(k_ref.dtype)


def project_queries_keys(block_ids, tokens, w_query, w_key):
    rows = tokens.shape[0]
    cols = w_query.shape[1]
    return pl.pallas_call(
        query_key_kernel,
        in_specs=[pl.BlockSpec(memory_space=SMEM)] + [pl.BlockSpec(memory_space=HBM)] * 3,
        out_specs=[pl.BlockSpec(memory_space=VMEM)] * 2,
        out_shape=[
            pltpu.HBM((rows, cols), jnp.bfloat16),
            in_vmem((1, rows + PAD, cols), jnp.bfloat16),
        ],
        scratch_shapes=[
            pltpu.VMEM(tokens.shape, jnp.bfloat16),
            pltpu.VMEM(w_query.shape, jnp.bfloat16),
            pltpu.VMEM(w_key.shape, jnp.bfloat16),
            pltpu.SemaphoreType.DMA((3, CHUNKS)),
        ],
        compiler_params=GRANT,
        name="project_queries_keys",
    )(off_chip(block_ids), off_chip(tokens), off_chip(w_query), off_chip(w_key))


def mix_kernel(u_ref, w_in_ref, w_out_ref, out_ref, wide_ref):
    count = u_ref.shape[1]
    hidden_units = w_in_ref.shape[0] // 2
    wide_ref[...] = u_ref[...].astype(jnp.float32)
    flat = jnp.concatenate([wide_ref[:, t, :] for t in range(count)], axis=1)
    parts = jnp.dot(w_in_ref[...], flat.astype(jnp.bfloat16), preferred_element_type=jnp.float32)
    hidden = (jax.nn.silu(parts[:hidden_units]) * parts[hidden_units:]).astype(jnp.bfloat16)
    mixed = flat + jnp.dot(w_out_ref[...], hidden, preferred_element_type=jnp.float32)
    for t in range(count):
        wide_ref[:, t, :] = mixed[:, t * HEAD_DIM : (t + 1) * HEAD_DIM]
    out_ref[...] = wide_ref[...].astype(out_ref.dtype)


def mix(gathered, w_in, w_out):
    return pl.pallas_call(
        mix_kernel,
        in_specs=[pl.BlockSpec(memory_space=VMEM)] * 3,
        out_specs=pl.BlockSpec(memory_space=VMEM),
        out_shape=in_vmem(gathered.shape, jnp.bfloat16),
        scratch_shapes=[pltpu.VMEM(gathered.shape, jnp.float32)],
        compiler_params=GRANT,
        name="mix_heads",
    )(on_chip(gathered), w_in, w_out)


def weight_kernel(ids_ref, q_ref, *refs):
    *key_refs, w_ref, total_ref, s_ref = refs
    half = q_ref.shape[0] // 2
    rows = q_ref.shape[0]
    chunk = 2 * half
    scale = HEAD_DIM ** (-0.5)
    q_row = lax.broadcasted_iota(jnp.int32, (half, 1), 0)
    lane = lax.broadcasted_iota(jnp.int32, (1, chunk), 1)
    lane_off = lane % BLK
    lane_blk = lane // BLK
    sources = [(k_ref, d) for k_ref in key_refs for d in range(k_ref.shape[0])]
    for s in range(2):
        id_lo, id_hi = ids_ref[2 * s], ids_ref[2 * s + 1]
        q_pos = jnp.where(q_row < BLK, id_lo * BLK + q_row, id_hi * BLK + q_row - BLK)
        queries = q_ref[s * half : (s + 1) * half, :]
        top = jnp.full((half, chunk), -1e30, jnp.float32)
        at = 0
        for first in range(0, len(sources), 2):
            pair = sources[first : first + 2]
            keys = jnp.concatenate(
                [k_ref[d, s * half : (s + 1) * half, :] for k_ref, d in pair], axis=0
            )
            k_ids = jnp.zeros((1, chunk), jnp.float32)
            for e, (k_ref, d) in enumerate(pair):
                tail = k_ref[d, rows:, :].astype(jnp.float32)
                for j in range(2):
                    wide = jnp.concatenate([tail[2 * s + j : 2 * s + j + 1, :]] * 3, axis=1)
                    k_ids = jnp.where(lane_blk == 2 * e + j, wide, k_ids)
            k_pos = k_ids.astype(jnp.int32) * BLK + lane_off
            scores = (
                lax.dot_general(
                    queries, keys, (((1,), (1,)), ((), ())), preferred_element_type=jnp.float32
                )
                * scale
            )
            scores = jnp.where(k_pos <= q_pos, scores, -1e30)
            s_ref[:, at : at + chunk] = scores
            top = jnp.maximum(top, scores)
            at += chunk
        top = jnp.max(top, axis=1, keepdims=True)
        total = jnp.zeros((half, chunk), jnp.float32)
        for at in range(0, s_ref.shape[1], chunk):
            weights = jnp.exp(s_ref[:, at : at + chunk] - top)
            total = total + weights
            w_ref[s, :, at : at + chunk] = weights.astype(w_ref.dtype)
        total = jnp.sum(total, axis=1, keepdims=True)
        total_ref[s * half : (s + 1) * half, :] = jnp.broadcast_to(total, (half, HEAD_DIM))


def attention_weights(block_ids, queries, keys):
    rows = queries.shape[0]
    half = rows // 2
    count = sum(piece.shape[0] for piece in keys) * half
    return pl.pallas_call(
        weight_kernel,
        in_specs=[pl.BlockSpec(memory_space=SMEM)]
        + [pl.BlockSpec(memory_space=VMEM)] * (1 + len(keys)),
        out_specs=[pl.BlockSpec(memory_space=VMEM)] * 2,
        out_shape=[
            in_vmem((2, half, count), jnp.bfloat16),
            pltpu.HBM((rows, HEAD_DIM), jnp.float32),
        ],
        scratch_shapes=[pltpu.VMEM((half, count), jnp.float32)],
        compiler_params=GRANT,
        name="attention_weights",
    )(off_chip(block_ids), off_chip(queries), *[on_chip(k) for k in keys])


def summed(w_ref, v_ref, s, first):
    half = w_ref.shape[1]
    sources = 4
    mine = lax.axis_index("context") // 2
    acc = jnp.zeros((half, HEAD_DIM), jnp.float32)
    for d in range(0, v_ref.shape[0], sources):
        spots = [mine ^ (2 * STEPS[e // 2] + e % 2) for e in range(d, d + sources)]
        values = jnp.concatenate(
            [v_ref[spot, s * half : (s + 1) * half, :] for spot in spots], axis=0
        )
        at = first + d * half
        acc = acc + jnp.dot(
            w_ref[s, :, at : at + sources * half], values, preferred_element_type=jnp.float32
        )
    return acc


def first_kernel(w_ref, total_ref, v_ref, part_ref, kept_ref):
    half = w_ref.shape[1]
    for s in range(2):
        part_ref[s * half : (s + 1) * half, :] = summed(w_ref, v_ref, s, 0)
    kept_ref[...] = total_ref[...]


def last_kernel(w_ref, total_ref, part_ref, v_ref, out_ref):
    half = w_ref.shape[1]
    for s in range(2):
        rows = slice(s * half, (s + 1) * half)
        acc = part_ref[rows, :] + summed(w_ref, v_ref, s, w_ref.shape[2] // 2)
        out_ref[rows, :] = (acc / total_ref[rows, :]).astype(out_ref.dtype)


def apply_first(weights, total, values):
    return pl.pallas_call(
        first_kernel,
        in_specs=[pl.BlockSpec(memory_space=VMEM)] * 3,
        out_specs=[pl.BlockSpec(memory_space=VMEM)] * 2,
        out_shape=[in_vmem(total.shape, jnp.float32)] * 2,
        compiler_params=GRANT,
        name="apply_first",
    )(weights, off_chip(total), on_chip(values))


def apply_last(weights, total, part, values):
    return pl.pallas_call(
        last_kernel,
        in_specs=[pl.BlockSpec(memory_space=VMEM)] * 4,
        out_specs=pl.BlockSpec(memory_space=VMEM),
        out_shape=jax.ShapeDtypeStruct(total.shape, jnp.bfloat16),
        compiler_params=GRANT,
        name="apply_last",
    )(weights, total, part, on_chip(values))


def pack_kernel(*refs):
    *pieces, out_ref = refs
    n = 0
    for piece in pieces:
        out_ref[n : n + piece.shape[0]] = piece[...]
        n += piece.shape[0]


def pack(*pieces):
    count = sum(piece.shape[0] for piece in pieces)
    return pl.pallas_call(
        pack_kernel,
        in_specs=[pl.BlockSpec(memory_space=VMEM)] * len(pieces),
        out_specs=pl.BlockSpec(memory_space=VMEM),
        out_shape=in_vmem((count, *pieces[0].shape[1:]), pieces[0].dtype),
        compiler_params=GRANT,
        name="pack",
    )(*[on_chip(piece) for piece in pieces])


def repeat_kernel(x_ref, out_ref, sems):
    copies = [
        pltpu.make_async_copy(x_ref, out_ref.at[n], sems.at[n]) for n in range(out_ref.shape[0])
    ]
    for copy in copies:
        copy.start()
    for copy in copies:
        copy.wait()


def repeat(x, count):
    return pl.pallas_call(
        repeat_kernel,
        in_specs=[pl.BlockSpec(memory_space=VMEM)],
        out_specs=pl.BlockSpec(memory_space=HBM),
        out_shape=pltpu.HBM((count, *x.shape), x.dtype),
        scratch_shapes=[pltpu.SemaphoreType.DMA((count,))],
        compiler_params=GRANT,
        name="repeat",
    )(on_chip(x))


def shards(tokens, w_query, w_key, w_value, mix_gate, mix_up, mix_down, block_ids):
    heads = mix_gate.shape[0]
    rows = tokens.shape[0]

    def exchange(x):
        return lax.all_to_all(x, "tensor", split_axis=0, concat_axis=0, tiled=True)

    def spread(x):
        return lax.all_to_all(
            x, "context", split_axis=0, concat_axis=0, axis_index_groups=CORE_GROUPS, tiled=True
        )

    def flip(x, bit):
        return lax.ppermute(x, "context", [(i, i ^ bit) for i in range(16)])

    w_in = jnp.concatenate([mix_gate, mix_up], axis=1).T
    w_out = mix_down.T
    values = project_values(tokens, w_value)
    gathered = exchange(values.reshape(heads, rows // heads, HEAD_DIM))
    tokens, values = lax.optimization_barrier((tokens, values))
    queries, own = project_queries_keys(block_ids, tokens, w_query, w_key)
    beside = flip(own, 2)
    mixed = mix(gathered, w_in, w_out)
    mixed_rows = exchange(mixed).reshape(rows, HEAD_DIM)
    pair = pack(own, beside)
    near = flip(pair, 4)
    wrap = flip(pair, 12)
    far = flip(pair, 8)
    keys = pack(pair, near, wrap, far)
    other_keys = flip(keys, 1)
    weights, total = attention_weights(block_ids, queries, [keys, other_keys])
    copies = repeat(mixed_rows, 8)
    values_mine = spread(copies)
    values_other = flip(values_mine, 1)
    part, total = apply_first(weights, total, values_mine)
    return apply_last(weights, total, part, values_other)


def solution(mesh):
    in_specs = (
        P("context", None),
        P(None, "tensor"),
        P(None, "tensor"),
        P(None, "tensor"),
        P(),
        P(),
        P(),
        P("context"),
    )
    out_specs = P("context", "tensor")
    return jax.shard_map(shards, mesh=mesh, in_specs=in_specs, out_specs=out_specs, check_vma=False)
```

```python
import jax
import jax.numpy as jnp
from jax import lax
from jax.experimental import pallas as pl
from jax.experimental.pallas import tpu as pltpu
from jax.sharding import PartitionSpec as P


HEAD_DIM = 128
BLK = 96
PAD = 16
CHUNKS = 8
STEPS = (0, 1, 3, 2)
CORE_GROUPS = [[2 * k + core for k in range(8)] for core in range(2)]
VMEM = pltpu.MemorySpace.VMEM
SMEM = pltpu.MemorySpace.SMEM
HBM = pltpu.MemorySpace.HBM
GRANT = pltpu.CompilerParams(vmem_limit_bytes=16 * 2**20)


def on_chip(x):
    return pltpu.with_memory_space_constraint(x, VMEM)


def off_chip(x):
    return pltpu.with_memory_space_constraint(x, HBM)


def in_vmem(shape, dtype):
    return pltpu.VMEM(shape, dtype)


def product(x_ref, kept, rest, refs, held, sems, fetch_kept):
    rows, width = x_ref.shape
    depth = width // CHUNKS
    half = CHUNKS // 2
    third = rows // 3

    def copies(k):
        at = pl.ds(k * depth, depth)
        found = [
            pltpu.make_async_copy(ref.at[at, :], keep.at[at, :], sems.at[n, k])
            for n, (ref, keep) in enumerate(zip(refs, held))
        ]
        if fetch_kept or k >= half:
            part = kept if k < half else rest
            to = pl.ds(k % half * depth, depth)
            found.append(pltpu.make_async_copy(x_ref.at[:, at], part.at[:, to], sems.at[2, k]))
        return found

    for k in range(CHUNKS):
        for copy in copies(k):
            copy.start()
    totals = [None] * 3
    for k in range(CHUNKS):
        for copy in copies(k):
            copy.wait()
        at = slice(k * depth, (k + 1) * depth)
        to = slice(k % half * depth, (k % half + 1) * depth)
        part = kept if k < half else rest
        sides = [keep[at, :] for keep in held]
        side = sides[0] if len(sides) == 1 else jnp.concatenate(sides, axis=1)
        for n in range(3):
            here = jnp.dot(
                part[n * third : (n + 1) * third, to], side, preferred_element_type=jnp.float32
            )
            totals[n] = here if totals[n] is None else totals[n] + here
    return jnp.concatenate(totals, axis=0)


def value_kernel(x_ref, w_ref, out_ref, kept_ref, rest, w_held, sems):
    total = product(x_ref, kept_ref, rest, [w_ref], [w_held], sems, True)
    out_ref[...] = total.astype(out_ref.dtype)


def project_values(tokens, w_value):
    rows, width = tokens.shape
    cols = w_value.shape[1]
    return pl.pallas_call(
        value_kernel,
        in_specs=[pl.BlockSpec(memory_space=HBM)] * 2,
        out_specs=[pl.BlockSpec(memory_space=VMEM)] * 2,
        out_shape=[
            in_vmem((rows, cols), jnp.bfloat16),
            in_vmem((rows, width // 2), jnp.bfloat16),
        ],
        scratch_shapes=[
            pltpu.VMEM((rows, width // 2), jnp.bfloat16),
            pltpu.VMEM(w_value.shape, jnp.bfloat16),
            pltpu.SemaphoreType.DMA((3, CHUNKS)),
        ],
        compiler_params=GRANT,
        name="project_values",
    )(off_chip(tokens), off_chip(w_value))


def query_key_kernel(
    ids_ref, x_ref, kept_ref, wq_ref, wk_ref, q_ref, k_ref, rest, q_held, k_held, sems
):
    rows, cols = q_ref.shape
    total = product(x_ref, kept_ref, rest, [wq_ref, wk_ref], [q_held, k_held], sems, False)
    q_ref[...] = total[:, :cols].astype(q_ref.dtype)
    k_ref[0, :rows, :] = total[:, cols:].astype(k_ref.dtype)
    row = lax.broadcasted_iota(jnp.int32, (PAD, cols), 0)
    ids = jnp.zeros((PAD, cols), jnp.float32)
    for j in range(4):
        ids = jnp.where(row == j, ids_ref[j].astype(jnp.float32), ids)
    k_ref[0, rows:, :] = ids.astype(k_ref.dtype)


def project_queries_keys(block_ids, tokens, kept, w_query, w_key):
    rows, width = tokens.shape
    cols = w_query.shape[1]
    return pl.pallas_call(
        query_key_kernel,
        in_specs=[
            pl.BlockSpec(memory_space=space) for space in (SMEM, HBM, VMEM, HBM, HBM)
        ],
        out_specs=[pl.BlockSpec(memory_space=VMEM)] * 2,
        out_shape=[
            pltpu.HBM((rows, cols), jnp.bfloat16),
            in_vmem((1, rows + PAD, cols), jnp.bfloat16),
        ],
        scratch_shapes=[
            pltpu.VMEM((rows, width // 2), jnp.bfloat16),
            pltpu.VMEM(w_query.shape, jnp.bfloat16),
            pltpu.VMEM(w_key.shape, jnp.bfloat16),
            pltpu.SemaphoreType.DMA((3, CHUNKS)),
        ],
        compiler_params=GRANT,
        name="project_queries_keys",
    )(off_chip(block_ids), off_chip(tokens), on_chip(kept), off_chip(w_query), off_chip(w_key))


def mix_kernel(u_ref, w_in_ref, w_out_ref, out_ref, wide_ref):
    count = u_ref.shape[1]
    hidden_units = w_in_ref.shape[0] // 2
    wide_ref[...] = u_ref[...].astype(jnp.float32)
    for first in range(0, count, 2):
        flat = jnp.concatenate([wide_ref[:, first + t, :] for t in range(2)], axis=1)
        parts = jnp.dot(
            w_in_ref[...], flat.astype(jnp.bfloat16), preferred_element_type=jnp.float32
        )
        hidden = (jax.nn.silu(parts[:hidden_units]) * parts[hidden_units:]).astype(jnp.bfloat16)
        mixed = flat + jnp.dot(w_out_ref[...], hidden, preferred_element_type=jnp.float32)
        for t in range(2):
            wide_ref[:, first + t, :] = mixed[:, t * HEAD_DIM : (t + 1) * HEAD_DIM]
    out_ref[...] = wide_ref[...].astype(out_ref.dtype)


def mix(gathered, w_in, w_out):
    return pl.pallas_call(
        mix_kernel,
        in_specs=[pl.BlockSpec(memory_space=VMEM)] * 3,
        out_specs=pl.BlockSpec(memory_space=VMEM),
        out_shape=in_vmem(gathered.shape, jnp.bfloat16),
        scratch_shapes=[pltpu.VMEM(gathered.shape, jnp.float32)],
        compiler_params=GRANT,
        name="mix_heads",
    )(on_chip(gathered), w_in, w_out)


def weight_kernel(ids_ref, q_ref, *refs):
    *key_refs, w_ref, total_ref, s_ref = refs
    half = q_ref.shape[0] // 2
    rows = q_ref.shape[0]
    chunk = 2 * half
    scale = HEAD_DIM ** (-0.5)
    q_row = lax.broadcasted_iota(jnp.int32, (half, 1), 0)
    lane = lax.broadcasted_iota(jnp.int32, (1, chunk), 1)
    lane_off = lane % BLK
    lane_blk = lane // BLK
    sources = [(k_ref, d) for k_ref in key_refs for d in range(k_ref.shape[0])]
    for s in range(2):
        id_lo, id_hi = ids_ref[2 * s], ids_ref[2 * s + 1]
        q_pos = jnp.where(q_row < BLK, id_lo * BLK + q_row, id_hi * BLK + q_row - BLK)
        queries = q_ref[s * half : (s + 1) * half, :]
        top = jnp.full((half, chunk), -1e30, jnp.float32)
        at = 0
        for first in range(0, len(sources), 2):
            pair = sources[first : first + 2]
            keys = jnp.concatenate(
                [k_ref[d, s * half : (s + 1) * half, :] for k_ref, d in pair], axis=0
            )
            k_ids = jnp.zeros((1, chunk), jnp.float32)
            for e, (k_ref, d) in enumerate(pair):
                tail = k_ref[d, rows:, :].astype(jnp.float32)
                for j in range(2):
                    wide = jnp.concatenate([tail[2 * s + j : 2 * s + j + 1, :]] * 3, axis=1)
                    k_ids = jnp.where(lane_blk == 2 * e + j, wide, k_ids)
            k_pos = k_ids.astype(jnp.int32) * BLK + lane_off
            scores = (
                lax.dot_general(
                    queries, keys, (((1,), (1,)), ((), ())), preferred_element_type=jnp.float32
                )
                * scale
            )
            scores = jnp.where(k_pos <= q_pos, scores, -1e30)
            s_ref[:, at : at + chunk] = scores
            top = jnp.maximum(top, scores)
            at += chunk
        top = jnp.max(top, axis=1, keepdims=True)
        total = jnp.zeros((half, chunk), jnp.float32)
        for at in range(0, s_ref.shape[1], chunk):
            weights = jnp.exp(s_ref[:, at : at + chunk] - top)
            total = total + weights
            w_ref[s, :, at : at + chunk] = weights.astype(w_ref.dtype)
        total = jnp.sum(total, axis=1, keepdims=True)
        total_ref[s * half : (s + 1) * half, :] = jnp.broadcast_to(total, (half, HEAD_DIM))


def attention_weights(block_ids, queries, keys):
    rows = queries.shape[0]
    half = rows // 2
    count = sum(piece.shape[0] for piece in keys) * half
    return pl.pallas_call(
        weight_kernel,
        in_specs=[pl.BlockSpec(memory_space=SMEM)]
        + [pl.BlockSpec(memory_space=VMEM)] * (1 + len(keys)),
        out_specs=[pl.BlockSpec(memory_space=VMEM)] * 2,
        out_shape=[
            in_vmem((2, half, count), jnp.bfloat16),
            pltpu.HBM((rows, HEAD_DIM), jnp.float32),
        ],
        scratch_shapes=[pltpu.VMEM((half, count), jnp.float32)],
        compiler_params=GRANT,
        name="attention_weights",
    )(off_chip(block_ids), off_chip(queries), *[on_chip(k) for k in keys])


def summed(w_ref, v_ref, s, first):
    half = w_ref.shape[1]
    sources = 4
    mine = lax.axis_index("context") // 2
    acc = jnp.zeros((half, HEAD_DIM), jnp.float32)
    for d in range(0, v_ref.shape[0], sources):
        spots = [mine ^ (2 * STEPS[e // 2] + e % 2) for e in range(d, d + sources)]
        values = jnp.concatenate(
            [v_ref[spot, s * half : (s + 1) * half, :] for spot in spots], axis=0
        )
        at = first + d * half
        acc = acc + jnp.dot(
            w_ref[s, :, at : at + sources * half], values, preferred_element_type=jnp.float32
        )
    return acc


def first_kernel(w_ref, total_ref, v_ref, part_ref, kept_ref):
    half = w_ref.shape[1]
    for s in range(2):
        part_ref[s * half : (s + 1) * half, :] = summed(w_ref, v_ref, s, 0)
    kept_ref[...] = total_ref[...]


def last_kernel(w_ref, total_ref, part_ref, v_ref, out_ref):
    half = w_ref.shape[1]
    for s in range(2):
        rows = slice(s * half, (s + 1) * half)
        acc = part_ref[rows, :] + summed(w_ref, v_ref, s, w_ref.shape[2] // 2)
        out_ref[rows, :] = (acc / total_ref[rows, :]).astype(out_ref.dtype)


def apply_first(weights, total, values):
    return pl.pallas_call(
        first_kernel,
        in_specs=[pl.BlockSpec(memory_space=VMEM)] * 3,
        out_specs=[pl.BlockSpec(memory_space=VMEM)] * 2,
        out_shape=[in_vmem(total.shape, jnp.float32)] * 2,
        compiler_params=GRANT,
        name="apply_first",
    )(weights, off_chip(total), on_chip(values))


def apply_last(weights, total, part, values):
    return pl.pallas_call(
        last_kernel,
        in_specs=[pl.BlockSpec(memory_space=VMEM)] * 4,
        out_specs=pl.BlockSpec(memory_space=VMEM),
        out_shape=jax.ShapeDtypeStruct(total.shape, jnp.bfloat16),
        compiler_params=GRANT,
        name="apply_last",
    )(weights, total, part, on_chip(values))


def pack_kernel(*refs):
    *pieces, out_ref = refs
    n = 0
    for piece in pieces:
        out_ref[n : n + piece.shape[0]] = piece[...]
        n += piece.shape[0]


def pack(*pieces):
    count = sum(piece.shape[0] for piece in pieces)
    return pl.pallas_call(
        pack_kernel,
        in_specs=[pl.BlockSpec(memory_space=VMEM)] * len(pieces),
        out_specs=pl.BlockSpec(memory_space=VMEM),
        out_shape=in_vmem((count, *pieces[0].shape[1:]), pieces[0].dtype),
        compiler_params=GRANT,
        name="pack",
    )(*[on_chip(piece) for piece in pieces])


def repeat_kernel(x_ref, out_ref, sems):
    copies = [
        pltpu.make_async_copy(x_ref, out_ref.at[n], sems.at[n]) for n in range(out_ref.shape[0])
    ]
    for copy in copies:
        copy.start()
    for copy in copies:
        copy.wait()


def repeat(x, count):
    return pl.pallas_call(
        repeat_kernel,
        in_specs=[pl.BlockSpec(memory_space=VMEM)],
        out_specs=pl.BlockSpec(memory_space=HBM),
        out_shape=pltpu.HBM((count, *x.shape), x.dtype),
        scratch_shapes=[pltpu.SemaphoreType.DMA((count,))],
        compiler_params=GRANT,
        name="repeat",
    )(on_chip(x))


def shards(tokens, w_query, w_key, w_value, mix_gate, mix_up, mix_down, block_ids):
    heads = mix_gate.shape[0]
    rows = tokens.shape[0]

    def exchange(x):
        return lax.all_to_all(x, "tensor", split_axis=0, concat_axis=0, tiled=True)

    def spread(x):
        return lax.all_to_all(
            x, "context", split_axis=0, concat_axis=0, axis_index_groups=CORE_GROUPS, tiled=True
        )

    def flip(x, bit):
        return lax.ppermute(x, "context", [(i, i ^ bit) for i in range(16)])

    w_in = jnp.concatenate([mix_gate, mix_up], axis=1).T
    w_out = mix_down.T
    values, kept = project_values(tokens, w_value)
    gathered = exchange(values.reshape(heads, rows // heads, HEAD_DIM))
    queries, own = project_queries_keys(block_ids, tokens, kept, w_query, w_key)
    beside = flip(own, 2)
    mixed = mix(gathered, w_in, w_out)
    mixed_rows = exchange(mixed).reshape(rows, HEAD_DIM)
    pair = pack(own, beside)
    near = flip(pair, 4)
    wrap = flip(pair, 12)
    far = flip(pair, 8)
    keys = pack(pair, near, wrap, far)
    other_keys = flip(keys, 1)
    weights, total = attention_weights(block_ids, queries, [keys, other_keys])
    copies = repeat(mixed_rows, 8)
    values_mine = spread(copies)
    values_other = flip(values_mine, 1)
    part, total = apply_first(weights, total, values_mine)
    return apply_last(weights, total, part, values_other)


def solution(mesh):
    in_specs = (
        P("context", None),
        P(None, "tensor"),
        P(None, "tensor"),
        P(None, "tensor"),
        P(),
        P(),
        P(),
        P("context"),
    )
    out_specs = P("context", "tensor")
    return jax.shard_map(shards, mesh=mesh, in_specs=in_specs, out_specs=out_specs, check_vma=False)
```

```python
import jax
import jax.numpy as jnp
from jax import lax
from jax.experimental import pallas as pl
from jax.experimental.pallas import tpu as pltpu
from jax.sharding import PartitionSpec as P


HEAD_DIM = 128
BLK = 96
PAD = 16
CHUNKS = 8
STEPS = (0, 1, 3, 2)
CORE_GROUPS = [[2 * k + core for k in range(8)] for core in range(2)]
VMEM = pltpu.MemorySpace.VMEM
SMEM = pltpu.MemorySpace.SMEM
HBM = pltpu.MemorySpace.HBM
GRANT = pltpu.CompilerParams(vmem_limit_bytes=16 * 2**20)


def on_chip(x):
    return pltpu.with_memory_space_constraint(x, VMEM)


def off_chip(x):
    return pltpu.with_memory_space_constraint(x, HBM)


def in_vmem(shape, dtype):
    return pltpu.VMEM(shape, dtype)


def product(x_ref, kept, rest, refs, held, sems, fetch_kept):
    rows, width = x_ref.shape
    depth = width // CHUNKS
    half = CHUNKS // 2
    third = rows // 3

    def copies(k):
        at = pl.ds(k * depth, depth)
        found = [
            pltpu.make_async_copy(ref.at[at, :], keep.at[at, :], sems.at[n, k])
            for n, (ref, keep) in enumerate(zip(refs, held))
        ]
        if fetch_kept or k >= half:
            part = kept if k < half else rest
            to = pl.ds(k % half * depth, depth)
            found.append(pltpu.make_async_copy(x_ref.at[:, at], part.at[:, to], sems.at[2, k]))
        return found

    for k in range(CHUNKS):
        for copy in copies(k):
            copy.start()
    totals = [None] * 3
    for k in range(CHUNKS):
        for copy in copies(k):
            copy.wait()
        at = slice(k * depth, (k + 1) * depth)
        to = slice(k % half * depth, (k % half + 1) * depth)
        part = kept if k < half else rest
        sides = [keep[at, :] for keep in held]
        side = sides[0] if len(sides) == 1 else jnp.concatenate(sides, axis=1)
        for n in range(3):
            here = jnp.dot(
                part[n * third : (n + 1) * third, to], side, preferred_element_type=jnp.float32
            )
            totals[n] = here if totals[n] is None else totals[n] + here
    return jnp.concatenate(totals, axis=0)


def value_kernel(x_ref, w_ref, out_ref, kept_ref, rest, w_held, sems):
    total = product(x_ref, kept_ref, rest, [w_ref], [w_held], sems, True)
    out_ref[...] = total.astype(out_ref.dtype)


def project_values(tokens, w_value):
    rows, width = tokens.shape
    cols = w_value.shape[1]
    return pl.pallas_call(
        value_kernel,
        in_specs=[pl.BlockSpec(memory_space=HBM)] * 2,
        out_specs=[pl.BlockSpec(memory_space=VMEM)] * 2,
        out_shape=[
            in_vmem((rows, cols), jnp.bfloat16),
            in_vmem((rows, width // 2), jnp.bfloat16),
        ],
        scratch_shapes=[
            pltpu.VMEM((rows, width // 2), jnp.bfloat16),
            pltpu.VMEM(w_value.shape, jnp.bfloat16),
            pltpu.SemaphoreType.DMA((3, CHUNKS)),
        ],
        compiler_params=GRANT,
        name="project_values",
    )(off_chip(tokens), off_chip(w_value))


def query_key_kernel(
    ids_ref, x_ref, kept_ref, wq_ref, wk_ref, q_ref, k_ref, rest, q_held, k_held, sems
):
    rows, cols = q_ref.shape
    total = product(x_ref, kept_ref, rest, [wq_ref, wk_ref], [q_held, k_held], sems, False)
    q_ref[...] = total[:, :cols].astype(q_ref.dtype)
    k_ref[0, :rows, :] = total[:, cols:].astype(k_ref.dtype)
    row = lax.broadcasted_iota(jnp.int32, (PAD, cols), 0)
    ids = jnp.zeros((PAD, cols), jnp.float32)
    for j in range(4):
        ids = jnp.where(row == j, ids_ref[j].astype(jnp.float32), ids)
    k_ref[0, rows:, :] = ids.astype(k_ref.dtype)


def project_queries_keys(block_ids, tokens, kept, w_query, w_key):
    rows, width = tokens.shape
    cols = w_query.shape[1]
    return pl.pallas_call(
        query_key_kernel,
        in_specs=[
            pl.BlockSpec(memory_space=space) for space in (SMEM, HBM, VMEM, HBM, HBM)
        ],
        out_specs=[pl.BlockSpec(memory_space=VMEM)] * 2,
        out_shape=[
            pltpu.HBM((rows, cols), jnp.bfloat16),
            in_vmem((1, rows + PAD, cols), jnp.bfloat16),
        ],
        scratch_shapes=[
            pltpu.VMEM((rows, width // 2), jnp.bfloat16),
            pltpu.VMEM(w_query.shape, jnp.bfloat16),
            pltpu.VMEM(w_key.shape, jnp.bfloat16),
            pltpu.SemaphoreType.DMA((3, CHUNKS)),
        ],
        compiler_params=GRANT,
        name="project_queries_keys",
    )(off_chip(block_ids), off_chip(tokens), on_chip(kept), off_chip(w_query), off_chip(w_key))


def mix_kernel(u_ref, w_in_ref, w_out_ref, out_ref, wide_ref):
    count = u_ref.shape[1]
    hidden_units = w_in_ref.shape[0] // 2
    wide_ref[...] = u_ref[...].astype(jnp.float32)
    flat = jnp.concatenate([wide_ref[:, t, :] for t in range(count)], axis=1)
    parts = jnp.dot(w_in_ref[...], flat.astype(jnp.bfloat16), preferred_element_type=jnp.float32)
    hidden = (jax.nn.silu(parts[:hidden_units]) * parts[hidden_units:]).astype(jnp.bfloat16)
    mixed = flat + jnp.dot(w_out_ref[...], hidden, preferred_element_type=jnp.float32)
    for t in range(count):
        wide_ref[:, t, :] = mixed[:, t * HEAD_DIM : (t + 1) * HEAD_DIM]
    out_ref[...] = wide_ref[...].astype(out_ref.dtype)


def mix(gathered, w_in, w_out):
    return pl.pallas_call(
        mix_kernel,
        in_specs=[pl.BlockSpec(memory_space=VMEM)] * 3,
        out_specs=pl.BlockSpec(memory_space=VMEM),
        out_shape=in_vmem(gathered.shape, jnp.bfloat16),
        scratch_shapes=[pltpu.VMEM(gathered.shape, jnp.float32)],
        compiler_params=GRANT,
        name="mix_heads",
    )(on_chip(gathered), w_in, w_out)


def weight_kernel(ids_ref, q_ref, *refs):
    *key_refs, w_ref, total_ref, s_ref = refs
    half = q_ref.shape[0] // 2
    rows = q_ref.shape[0]
    chunk = 2 * half
    scale = HEAD_DIM ** (-0.5)
    q_row = lax.broadcasted_iota(jnp.int32, (half, 1), 0)
    lane = lax.broadcasted_iota(jnp.int32, (1, chunk), 1)
    lane_off = lane % BLK
    lane_blk = lane // BLK
    sources = [(k_ref, d) for k_ref in key_refs for d in range(k_ref.shape[0])]
    for s in range(2):
        id_lo, id_hi = ids_ref[2 * s], ids_ref[2 * s + 1]
        q_pos = jnp.where(q_row < BLK, id_lo * BLK + q_row, id_hi * BLK + q_row - BLK)
        queries = q_ref[s * half : (s + 1) * half, :]
        top = jnp.full((half, chunk), -1e30, jnp.float32)
        at = 0
        for first in range(0, len(sources), 2):
            pair = sources[first : first + 2]
            keys = jnp.concatenate(
                [k_ref[d, s * half : (s + 1) * half, :] for k_ref, d in pair], axis=0
            )
            k_ids = jnp.zeros((1, chunk), jnp.float32)
            for e, (k_ref, d) in enumerate(pair):
                tail = k_ref[d, rows:, :].astype(jnp.float32)
                for j in range(2):
                    wide = jnp.concatenate([tail[2 * s + j : 2 * s + j + 1, :]] * 3, axis=1)
                    k_ids = jnp.where(lane_blk == 2 * e + j, wide, k_ids)
            k_pos = k_ids.astype(jnp.int32) * BLK + lane_off
            scores = (
                lax.dot_general(
                    queries, keys, (((1,), (1,)), ((), ())), preferred_element_type=jnp.float32
                )
                * scale
            )
            scores = jnp.where(k_pos <= q_pos, scores, -1e30)
            s_ref[:, at : at + chunk] = scores
            top = jnp.maximum(top, scores)
            at += chunk
        top = jnp.max(top, axis=1, keepdims=True)
        total = jnp.zeros((half, chunk), jnp.float32)
        for at in range(0, s_ref.shape[1], chunk):
            weights = jnp.exp(s_ref[:, at : at + chunk] - top)
            total = total + weights
            w_ref[s, :, at : at + chunk] = weights.astype(w_ref.dtype)
        total = jnp.sum(total, axis=1, keepdims=True)
        total_ref[s * half : (s + 1) * half, :] = jnp.broadcast_to(total, (half, HEAD_DIM))


def attention_weights(block_ids, queries, keys):
    rows = queries.shape[0]
    half = rows // 2
    count = sum(piece.shape[0] for piece in keys) * half
    return pl.pallas_call(
        weight_kernel,
        in_specs=[pl.BlockSpec(memory_space=SMEM)]
        + [pl.BlockSpec(memory_space=VMEM)] * (1 + len(keys)),
        out_specs=[pl.BlockSpec(memory_space=VMEM)] * 2,
        out_shape=[
            in_vmem((2, half, count), jnp.bfloat16),
            pltpu.HBM((rows, HEAD_DIM), jnp.float32),
        ],
        scratch_shapes=[pltpu.VMEM((half, count), jnp.float32)],
        compiler_params=GRANT,
        name="attention_weights",
    )(off_chip(block_ids), off_chip(queries), *[on_chip(k) for k in keys])


def summed(w_ref, v_ref, s, first):
    half = w_ref.shape[1]
    sources = 8
    mine = lax.axis_index("context") // 2
    acc = jnp.zeros((half, HEAD_DIM), jnp.float32)
    for d in range(0, v_ref.shape[0], sources):
        spots = [mine ^ (2 * STEPS[e // 2] + e % 2) for e in range(d, d + sources)]
        values = jnp.concatenate(
            [v_ref[spot, s * half : (s + 1) * half, :] for spot in spots], axis=0
        )
        at = first + d * half
        acc = acc + jnp.dot(
            w_ref[s, :, at : at + sources * half], values, preferred_element_type=jnp.float32
        )
    return acc


def first_kernel(w_ref, total_ref, v_ref, part_ref, kept_ref):
    half = w_ref.shape[1]
    for s in range(2):
        part_ref[s * half : (s + 1) * half, :] = summed(w_ref, v_ref, s, 0)
    kept_ref[...] = total_ref[...]


def last_kernel(w_ref, total_ref, part_ref, v_ref, out_ref):
    half = w_ref.shape[1]
    for s in range(2):
        rows = slice(s * half, (s + 1) * half)
        acc = part_ref[rows, :] + summed(w_ref, v_ref, s, w_ref.shape[2] // 2)
        out_ref[rows, :] = (acc / total_ref[rows, :]).astype(out_ref.dtype)


def apply_first(weights, total, values):
    return pl.pallas_call(
        first_kernel,
        in_specs=[pl.BlockSpec(memory_space=VMEM)] * 3,
        out_specs=[pl.BlockSpec(memory_space=VMEM)] * 2,
        out_shape=[in_vmem(total.shape, jnp.float32)] * 2,
        compiler_params=GRANT,
        name="apply_first",
    )(weights, off_chip(total), on_chip(values))


def apply_last(weights, total, part, values):
    return pl.pallas_call(
        last_kernel,
        in_specs=[pl.BlockSpec(memory_space=VMEM)] * 4,
        out_specs=pl.BlockSpec(memory_space=VMEM),
        out_shape=jax.ShapeDtypeStruct(total.shape, jnp.bfloat16),
        compiler_params=GRANT,
        name="apply_last",
    )(weights, total, part, on_chip(values))


def pack_kernel(*refs):
    *pieces, out_ref = refs
    n = 0
    for piece in pieces:
        out_ref[n : n + piece.shape[0]] = piece[...]
        n += piece.shape[0]


def pack(*pieces):
    count = sum(piece.shape[0] for piece in pieces)
    return pl.pallas_call(
        pack_kernel,
        in_specs=[pl.BlockSpec(memory_space=VMEM)] * len(pieces),
        out_specs=pl.BlockSpec(memory_space=VMEM),
        out_shape=in_vmem((count, *pieces[0].shape[1:]), pieces[0].dtype),
        compiler_params=GRANT,
        name="pack",
    )(*[on_chip(piece) for piece in pieces])


def repeat_kernel(x_ref, out_ref, sems):
    copies = [
        pltpu.make_async_copy(x_ref, out_ref.at[n], sems.at[n]) for n in range(out_ref.shape[0])
    ]
    for copy in copies:
        copy.start()
    for copy in copies:
        copy.wait()


def repeat(x, count):
    return pl.pallas_call(
        repeat_kernel,
        in_specs=[pl.BlockSpec(memory_space=VMEM)],
        out_specs=pl.BlockSpec(memory_space=HBM),
        out_shape=pltpu.HBM((count, *x.shape), x.dtype),
        scratch_shapes=[pltpu.SemaphoreType.DMA((count,))],
        compiler_params=GRANT,
        name="repeat",
    )(on_chip(x))


def shards(tokens, w_query, w_key, w_value, mix_gate, mix_up, mix_down, block_ids):
    heads = mix_gate.shape[0]
    rows = tokens.shape[0]

    def exchange(x):
        return lax.all_to_all(x, "tensor", split_axis=0, concat_axis=0, tiled=True)

    def spread(x):
        return lax.all_to_all(
            x, "context", split_axis=0, concat_axis=0, axis_index_groups=CORE_GROUPS, tiled=True
        )

    def flip(x, bit):
        return lax.ppermute(x, "context", [(i, i ^ bit) for i in range(16)])

    w_in = jnp.concatenate([mix_gate, mix_up], axis=1).T
    w_out = mix_down.T
    values, kept = project_values(tokens, w_value)
    gathered = exchange(values.reshape(heads, rows // heads, HEAD_DIM))
    queries, own = project_queries_keys(block_ids, tokens, kept, w_query, w_key)
    beside = flip(own, 2)
    mixed = mix(gathered, w_in, w_out)
    mixed_rows = exchange(mixed).reshape(rows, HEAD_DIM)
    pair = pack(own, beside)
    near = flip(pair, 4)
    wrap = flip(pair, 12)
    far = flip(pair, 8)
    keys = pack(pair, near, wrap, far)
    other_keys = flip(keys, 1)
    weights, total = attention_weights(block_ids, queries, [keys, other_keys])
    copies = repeat(mixed_rows, 8)
    values_mine = spread(copies)
    values_other = flip(values_mine, 1)
    part, total = apply_first(weights, total, values_mine)
    return apply_last(weights, total, part, values_other)


def solution(mesh):
    in_specs = (
        P("context", None),
        P(None, "tensor"),
        P(None, "tensor"),
        P(None, "tensor"),
        P(),
        P(),
        P(),
        P("context"),
    )
    out_specs = P("context", "tensor")
    return jax.shard_map(shards, mesh=mesh, in_specs=in_specs, out_specs=out_specs, check_vma=False)
```
